128 devices in a mesh: grp: 4 (over y), seq: 32 (over x, z, core).
Axes of the slice: x: 4, y: 4, z: 4, core: 2. Of those that a mesh axis runs over, the one named last changes fastest.
Arguments:
- points: bfloat16 [65536, 512], P(('grp', 'seq')), may hold values from -6 to 6
- pattern_first: int32 [1024, 3], P(('grp', 'seq')), may hold values from 0 to 255, as said below
- pattern_second: int32 [1024, 3], P(('grp', 'seq')), may hold values from 0 to 7
- destination: int32 [65536], P(('grp', 'seq')), may hold values from 0 to 65535, as said below
- norm_gains: float32 [4, 512], replicated, may hold values from 0.1 to 1.9
- w_qkv: bfloat16 [2, 512, 1536], replicated
- w_proj: bfloat16 [2, 512, 512], replicated, may hold values from -0.25 to 0.25
- w_up: bfloat16 [2, 512, 2048], replicated, may hold values from -0.25 to 0.25
- w_down: bfloat16 [2, 2048, 512], replicated, may hold values from -0.125 to 0.125
- w_head: bfloat16 [3, 512], replicated, may hold values from -0.25 to 0.25
Outputs:
- features: bfloat16 [65536, 512], P(('grp', 'seq'))
- normals: float32 [3, 65536], P(None, ('grp', 'seq'))
The draws below stay inside these ranges and needn't reach their ends.
Inputs may be any that keep to these rules, and one draw needn't show every extreme that they name: `pattern_first`: the 24 entries of the patches of one device name at most 2 patches (repeats counted) lying on any one device of the group, and exactly 2 on some device. `destination`: a permutation of the positions; the 512 points of one device place at most 8 points in any one block of 512 consecutive positions of the second order, and exactly 8 in some block for every device.
All inputs are finite; a program needn't handle non-finite values.
Results may differ from the reference program's by a relative error of at most 0.024.
Values may be sent and summed in bfloat16 or wider, within the bound.
A program may use at most 128 MiB of HBM per device.

```python
import math
import jax
import jax.numpy as jnp
from jax import lax

C = 512
HEADS = 8
FF = 2048
PATCH = 64
K_SEL = 3
ROWS_DEV = 512
PATCH_DEV = 8
N_PATCHES = 1024
N_POINTS = 65536
REQ = 2
N_GRP = 4
N_SEQ = 32


def draw_w_qkv(key, part):
    parts_keys = jax.random.split(key, 3)
    spread_qk = 2.0 / math.sqrt(C)
    queries = jax.random.normal(parts_keys[0], (2, C, C), jnp.float32) * spread_qk
    values = jax.random.normal(parts_keys[2], (2, C, C), jnp.float32) / math.sqrt(C)
    key_part = jax.random.normal(parts_keys[1], (2, C, C), jnp.float32) * spread_qk
    return jnp.concatenate([queries, key_part, values], axis=-1).astype(jnp.bfloat16)


def draw_pattern_first(key, part):
    devices = N_GRP * N_SEQ
    wanted = PATCH_DEV * K_SEL
    slots = N_SEQ * REQ
    device_keys = jax.random.split(key, devices)

    def one_device(sub):
        pieces = jax.random.split(sub, 4)
        favored = jax.random.randint(pieces[0], (), 0, N_SEQ)
        ranking = jax.random.permutation(pieces[1], slots).astype(jnp.int32)
        source = (jnp.arange(slots, dtype=jnp.int32) // REQ).astype(jnp.int32)
        scored = jnp.where(source == favored, ranking - slots, ranking)
        order = jnp.argsort(scored, stable=True)
        picked = source[order[:wanted]]
        picked = jax.random.permutation(pieces[2], picked)
        local = jax.random.randint(pieces[3], (wanted,), 0, PATCH_DEV)
        return (picked * PATCH_DEV + local).astype(jnp.int32)
    return jax.vmap(one_device)(device_keys).reshape(N_PATCHES, K_SEL).astype(jnp.int32)


def draw_destination(key, part):
    devices = N_GRP * N_SEQ
    per_peer = ROWS_DEV // devices
    parts_keys = jax.random.split(key, 5)
    levels = jnp.concatenate([jnp.full((devices // 4,), 2 * per_peer, jnp.int32), jnp.full((devices // 2,), per_peer, jnp.int32), jnp.zeros((devices - devices // 4 - devices // 2,), jnp.int32)])
    weights = jax.random.permutation(parts_keys[0], levels)
    ending = jnp.cumsum(weights)
    shifting = jax.random.permutation(parts_keys[1], devices)
    relabel = jax.random.permutation(parts_keys[2], devices)
    slots_src = jax.vmap(lambda sub: jax.random.permutation(sub, ROWS_DEV))(jax.random.split(parts_keys[3], devices))
    classes = jnp.sum((ending[None, None, :] <= slots_src[:, :, None]).astype(jnp.int32), axis=-1)
    target = relabel[(shifting[:, None] + classes) % devices]
    places = jax.vmap(lambda sub: jax.random.permutation(sub, ROWS_DEV))(jax.random.split(parts_keys[4], devices))
    return (target * ROWS_DEV + places[target, slots_src]).reshape(-1).astype(jnp.int32)


def with_ends(values, rng, smallest, high):
    index_at = [jax.random.randint(jax.random.fold_in(rng, axis), (), 0, length) for axis, length in enumerate(values.shape)]
    main_axis = values.shape.index(max(values.shape))
    beside = index_at[:main_axis] + [(index_at[main_axis] + 1) % values.shape[main_axis]] + index_at[main_axis + 1:]
    return values.at[tuple(index_at)].set(smallest).at[tuple(beside)].set(high)


def steps_of(stream_key, extent, cuts, smallest, high):
    def one(dim, parts):
        heights = jax.random.uniform(jax.random.fold_in(jax.random.fold_in(stream_key, 6), dim), (parts,), jnp.float32, smallest / len(cuts), high / len(cuts))
        return jnp.repeat(jnp.exp(heights), extent[dim] // parts).reshape((-1,) + (1,) * (len(extent) - dim - 1))

    level = one(*cuts[0])
    for cut in cuts[1:]:
        level = level * one(*cut)
    return level


def scatter_about(stream_key, shape, deviation, bound, cuts=(), held_as=jnp.bfloat16):
    values = jax.random.normal(stream_key, shape, jnp.float32) * deviation
    if len(cuts) > 0:
        values = steps_of(stream_key, shape, cuts, -0.22, 0.18) * values
    return jnp.clip(values, min=-bound, max=bound).astype(held_as)


def setup_inputs(seed: int = 0) -> dict:
    key_list = jax.random.split(jax.random.key(seed), 11)
    return {
        "points": scatter_about(key_list[0], (N_POINTS, C), 1.0, 6.0, ((0, 128),)),
        "pattern_first": draw_pattern_first(jax.random.fold_in(key_list[10], 71), 0),
        "pattern_second": with_ends(jax.random.randint(key_list[2], (N_PATCHES, K_SEL), 0, PATCH_DEV), jax.random.fold_in(key_list[2], 1), 0, PATCH_DEV - 1).astype(jnp.int32),
        "destination": draw_destination(jax.random.fold_in(key_list[10], 71), 0),
        "norm_gains": jnp.clip(1.0 + 0.18 * jax.random.normal(key_list[4], (4, C), jnp.float32), 0.1, 1.9),
        "w_qkv": draw_w_qkv(jax.random.fold_in(key_list[10], 71), 0),
        "w_proj": scatter_about(key_list[6], (2, C, C), C ** -0.5, 0.25),
        "w_up": scatter_about(key_list[7], (2, C, FF), C ** -0.5, 0.25),
        "w_down": scatter_about(key_list[8], (2, FF, C), FF ** -0.5, 0.125),
        "w_head": scatter_about(key_list[9], (3, C), C ** -0.5, 0.25),
    }


def layer_norm(rows, gains):
    values = rows.astype(jnp.float32)
    average = lax.optimization_barrier(jnp.mean(values, axis=-1, keepdims=True))
    spread = lax.optimization_barrier(jnp.mean((values - average) ** 2, axis=-1, keepdims=True))
    return (values - average) * lax.rsqrt(spread + 1e-05) * gains

def attend(queries, key_rows, value_rows):
    count = queries.shape[0]
    head_dim = C // HEADS
    qh = queries.reshape(count, PATCH, HEADS, head_dim).astype(jnp.float32)
    kh = key_rows.reshape(count, -1, HEADS, head_dim).astype(jnp.float32)
    vh = value_rows.reshape(count, -1, HEADS, head_dim).astype(jnp.float32)
    scores = jnp.einsum('nqhd,nkhd->nhqk', qh, kh) * head_dim ** (-0.5)
    probs = jax.nn.softmax(scores, axis=-1).astype(jnp.bfloat16)
    probs = lax.optimization_barrier(probs).astype(jnp.float32)
    mixed = jnp.einsum('nhqk,nkhd->nqhd', probs, vh)
    return mixed.reshape(count * PATCH, C).astype(jnp.bfloat16)

def block(rows, pattern, groups, section, norm_gains, w_qkv, w_proj, w_up, w_down):
    normed = layer_norm(rows, norm_gains[2 * section]).astype(jnp.bfloat16)
    proj = jnp.dot(normed, w_qkv[section], preferred_element_type=jnp.float32)
    queries = proj[:, :C].astype(jnp.bfloat16)
    key_rows = proj[:, C:2 * C].astype(jnp.bfloat16)
    value_rows = proj[:, 2 * C:].astype(jnp.bfloat16)
    per_group = rows.shape[0] // (groups * PATCH)
    qg = queries.reshape(groups, per_group, PATCH, C)
    kg = key_rows.reshape(groups, per_group, PATCH, C)
    vg = value_rows.reshape(groups, per_group, PATCH, C)
    pg = pattern.reshape(groups, per_group, K_SEL)

    def one_group(items):
        qq, kk, vv, chosen = items
        keys_all = jnp.concatenate([kk[:, None], kk[chosen]], axis=1).reshape(per_group, -1, C)
        vals_all = jnp.concatenate([vv[:, None], vv[chosen]], axis=1).reshape(per_group, -1, C)
        return attend(qq, keys_all, vals_all)
    attended = lax.map(one_group, (qg, kg, vg, pg)).reshape(-1, C)
    first = (rows.astype(jnp.float32) + jnp.dot(attended, w_proj[section], preferred_element_type=jnp.float32)).astype(jnp.bfloat16)
    hidden = layer_norm(first, norm_gains[2 * section + 1]).astype(jnp.bfloat16)
    upper = jnp.dot(hidden, w_up[section], preferred_element_type=jnp.float32)
    act = jax.nn.gelu(upper, approximate=False).astype(jnp.bfloat16)
    return (first.astype(jnp.float32) + jnp.dot(act, w_down[section], preferred_element_type=jnp.float32)).astype(jnp.bfloat16)

def reference(points, pattern_first, pattern_second, destination, norm_gains, w_qkv, w_proj, w_up, w_down, w_head):
    first = block(points, pattern_first, N_GRP, 0, norm_gains, w_qkv, w_proj, w_up, w_down)
    second = jnp.zeros_like(first).at[destination].set(first)
    features = block(second, pattern_second, N_GRP * N_SEQ, 1, norm_gains, w_qkv, w_proj, w_up, w_down)
    normals = lax.dot_general(w_head, features, (((1,), (1,)), ((), ())), preferred_element_type=jnp.float32)
    return (features, normals)
```

```python
import functools

import jax
import jax.numpy as jnp
from jax import lax
from jax.experimental import pallas as pl
from jax.experimental.pallas import tpu as pltpu
from jax.sharding import PartitionSpec as P

HEADS = 8
PATCH = 64
SLOTS = 8
GROUP_HEADS = 4
BF16 = jnp.bfloat16
F32 = jnp.float32


def norm(rows, gains):
    values = rows.astype(F32)
    centered = values - jnp.mean(values, axis=-1, keepdims=True)
    spread = jnp.mean(centered * centered, axis=-1, keepdims=True)
    return (centered * lax.rsqrt(spread + 1e-05) * gains).astype(BF16)


def mm(a, b):
    return jnp.dot(a, b, preferred_element_type=F32)


def attend_patch(queries, keys, values):
    width = GROUP_HEADS * PATCH
    lane = lax.broadcasted_iota(jnp.int32, (PATCH, width), 1) // PATCH
    mixed = []
    for part in range(HEADS // GROUP_HEADS):
        cols = slice(part * width, (part + 1) * width)
        q = queries[:, cols]
        spread = jnp.concatenate(
            [jnp.where(lane == head, q, jnp.zeros_like(q)) for head in range(GROUP_HEADS)], axis=0
        )
        scores = lax.dot_general(
            spread, keys[:, cols], (((1,), (1,)), ((), ())), preferred_element_type=F32
        )
        top = jnp.max(scores, axis=-1, keepdims=True)
        weights = jnp.exp((scores - top) * PATCH ** (-0.5))
        total = jnp.sum(weights, axis=-1, keepdims=True)
        out = mm(weights.astype(BF16), values[:, cols]) * (1.0 / total)
        acc = jnp.where(lane == 0, out[:PATCH], 0.0)
        for head in range(1, GROUP_HEADS):
            acc = acc + jnp.where(lane == head, out[head * PATCH : (head + 1) * PATCH], 0.0)
        mixed.append(acc)
    return jnp.concatenate(mixed, axis=1).astype(BF16)


def finish(rows, att_ref, gains, wp_ref, wu_ref, wd_ref, acc_ref, waits):
    waits[0]()
    first = (rows.astype(F32) + mm(att_ref[...], wp_ref[...])).astype(BF16)
    hidden = norm(first, gains)
    acc_ref[...] = first.astype(F32)
    waits[1]()
    waits[2]()
    ff = wu_ref.shape[1]
    step = 512
    for at in range(0, ff, step):
        upper = mm(hidden, wu_ref[:, at : at + step])
        act = (0.5 * upper * (1.0 + lax.erf(upper * 0.7071067811865476))).astype(BF16)
        acc_ref[...] += mm(act, wd_ref[at : at + step, :])
    return acc_ref[...].astype(BF16)


def weight_copies(block, sources, targets, sems):
    return [
        pltpu.make_async_copy(source.at[block], target, sems.at[n])
        for n, (source, target) in enumerate(zip(sources, targets))
    ]


def first_kernel(
    pattern, points, dest, gains, group, qkv_hbm, proj_hbm, up_hbm, down_hbm,
    out, chosen, q_ref, att_ref, acc_ref, wq, wp, wu, wd, sems, row_sems,
):
    copies = weight_copies(0, (qkv_hbm, proj_hbm, up_hbm, down_hbm), (wq, wp, wu, wd), sems)
    patches, picks = pattern.shape
    rows_here, channels = points.shape
    fetches = [
        pltpu.make_async_copy(
            group.at[pattern[p, j]],
            chosen.at[p, pl.ds((j + 1) * PATCH, PATCH)],
            row_sems.at[p * picks + j],
        )
        for p in range(patches)
        for j in range(picks)
    ]
    copies[0].start()
    for fetch in fetches:
        fetch.start()
    for copy in copies[1:]:
        copy.start()
    for p in range(patches):
        chosen[p, :PATCH] = points[p * PATCH : (p + 1) * PATCH]
    target = dest[...] >> 9
    devices = out.shape[0] // SLOTS
    on_device = lax.broadcasted_iota(jnp.int32, (devices, rows_here), 0) == target
    before = lax.broadcasted_iota(jnp.int32, (rows_here, rows_here), 0) < lax.broadcasted_iota(
        jnp.int32, (rows_here, rows_here), 1
    )
    earlier = mm(on_device.astype(BF16), before.astype(BF16))
    rank = jnp.sum(jnp.where(on_device, earlier, 0.0), axis=0, keepdims=True)
    slot = target * SLOTS + rank.astype(jnp.int32)
    gain = gains[0:1]
    copies[0].wait()
    q_ref[...] = mm(norm(points[...], gain), wq[:, :channels]).astype(BF16)
    for fetch in fetches:
        fetch.wait()

    def one(p, carry):
        hidden = norm(chosen[p], gain)
        kv = mm(hidden, wq[:, channels:]).astype(BF16)
        at = pl.multiple_of(p * PATCH, PATCH)
        att_ref[pl.ds(at, PATCH)] = attend_patch(
            q_ref[pl.ds(at, PATCH)], kv[:, :channels], kv[:, channels:]
        )
        return carry

    lax.fori_loop(0, patches, one, 0)
    done = finish(
        points[...], att_ref, gains[1:2], wp, wu, wd, acc_ref, [copy.wait for copy in copies[1:]]
    )
    step = 256
    for at in range(0, devices * SLOTS, step):
        match = lax.broadcasted_iota(jnp.int32, (step, rows_here), 0) + at == slot
        out[at : at + step] = mm(match.astype(BF16), done).astype(BF16)


def second_kernel(
    pattern, incoming, dest_all, gains, head, qkv_hbm, proj_hbm, up_hbm, down_hbm,
    features, normals, rows_ref, q_ref, kv_ref, att_ref, acc_ref, wq, wp, wu, wd, sems,
):
    copies = weight_copies(1, (qkv_hbm, proj_hbm, up_hbm, down_hbm), (wq, wp, wu, wd), sems)
    for copy in copies:
        copy.start()
    patches, picks = pattern.shape
    rows_here, channels = features.shape
    devices = dest_all.shape[0]
    slots = devices * SLOTS
    me = lax.axis_index("grp") * lax.axis_size("seq") + lax.axis_index("seq")
    dest = jnp.transpose(dest_all[...])
    mine = (dest >> 9) == me
    before = lax.broadcasted_iota(jnp.int32, (rows_here, rows_here), 0) > lax.broadcasted_iota(
        jnp.int32, (rows_here, rows_here), 1
    )
    rank = mm(before.astype(BF16), mine.astype(BF16)).astype(jnp.int32)
    place = jnp.where(mine, (dest & 511) + 1, 0)
    table = jnp.concatenate(
        [
            jnp.sum(jnp.where(rank == j, place, 0), axis=0, keepdims=True)
            for j in range(SLOTS)
        ],
        axis=0,
    )
    spread = (
        lax.broadcasted_iota(jnp.int32, (devices, slots), 1) // SLOTS
        == lax.broadcasted_iota(jnp.int32, (devices, slots), 0)
    ).astype(BF16)
    high = mm((table >> 4).astype(F32).astype(BF16), spread)
    low = mm((table & 15).astype(F32).astype(BF16), spread)
    of_rank = (
        lax.broadcasted_iota(jnp.int32, (SLOTS, slots), 1) % SLOTS
        == lax.broadcasted_iota(jnp.int32, (SLOTS, slots), 0)
    )
    slot_place = jnp.sum(
        jnp.where(of_rank, high * 16.0 + low, 0.0), axis=0, keepdims=True
    ).astype(jnp.int32)
    step = 256
    for at in range(0, rows_here, step):
        match = lax.broadcasted_iota(jnp.int32, (step, slots), 0) + (at + 1) == slot_place
        rows_ref[at : at + step] = mm(match.astype(BF16), incoming[...]).astype(BF16)
    copies[0].wait()
    hidden = norm(rows_ref[...], gains[2:3])
    q_ref[...] = mm(hidden, wq[:, :channels]).astype(BF16)
    kv_ref[...] = (
        mm(hidden, wq[:, channels:]).astype(BF16).reshape(patches, PATCH, 2 * channels)
    )

    def one(p, carry):
        kv = jnp.concatenate([kv_ref[p]] + [kv_ref[pattern[p, j]] for j in range(picks)], axis=0)
        at = pl.multiple_of(p * PATCH, PATCH)
        att_ref[pl.ds(at, PATCH)] = attend_patch(
            q_ref[pl.ds(at, PATCH)], kv[:, :channels], kv[:, channels:]
        )
        return carry

    lax.fori_loop(0, patches, one, 0)
    done = finish(
        rows_ref[...], att_ref, gains[3:4], wp, wu, wd, acc_ref, [copy.wait for copy in copies[1:]]
    )
    features[...] = done
    normals[...] = lax.dot_general(
        head[...], done, (((1,), (1,)), ((), ())), preferred_element_type=F32
    )


def shards(
    points, pattern_first, pattern_second, destination, norm_gains, w_qkv, w_proj, w_up, w_down, w_head
):
    rows_here, channels = points.shape
    patches = rows_here // PATCH
    ff = w_up.shape[2]
    devices = lax.axis_size("grp") * lax.axis_size("seq")
    slots = devices * SLOTS
    vmem = pl.BlockSpec(memory_space=pltpu.VMEM)
    smem = pl.BlockSpec(memory_space=pltpu.SMEM)
    anywhere = pl.BlockSpec(memory_space=pl.ANY)
    weights = [
        pltpu.VMEM((channels, 3 * channels), BF16),
        pltpu.VMEM((channels, channels), BF16),
        pltpu.VMEM((channels, ff), BF16),
        pltpu.VMEM((ff, channels), BF16),
        pltpu.SemaphoreType.DMA((4,)),
    ]
    params = pltpu.CompilerParams(vmem_limit_bytes=48 << 20)
    work = 2 * rows_here * channels * (4 * channels + 2 * ff)
    cost = pl.CostEstimate(flops=2 * work, bytes_accessed=8 << 20, transcendentals=rows_here * ff)
    group = lax.all_gather(points, "seq", axis=0, tiled=True).reshape(-1, PATCH, channels)
    dest_row = destination.reshape(1, rows_here)
    dest_all = lax.all_gather(dest_row, ("grp", "seq"), axis=0, tiled=True)
    outgoing = pl.pallas_call(
        first_kernel,
        out_shape=jax.ShapeDtypeStruct((slots, channels), BF16),
        in_specs=[smem, vmem, vmem, vmem] + [anywhere] * 5,
        out_specs=vmem,
        scratch_shapes=[
            pltpu.VMEM((patches, 4 * PATCH, channels), BF16),
            pltpu.VMEM((rows_here, channels), BF16),
            pltpu.VMEM((rows_here, channels), BF16),
            pltpu.VMEM((rows_here, channels), F32),
        ]
        + weights
        + [pltpu.SemaphoreType.DMA((patches * pattern_first.shape[1],))],
        compiler_params=params,
        cost_estimate=cost,
        name="first_block",
    )(pattern_first, points, dest_row, norm_gains, group, w_qkv, w_proj, w_up, w_down)
    incoming = lax.all_to_all(
        outgoing.reshape(devices, SLOTS, channels), ("grp", "seq"), split_axis=0, concat_axis=0, tiled=True
    ).reshape(slots, channels)
    features, normals = pl.pallas_call(
        second_kernel,
        out_shape=(
            jax.ShapeDtypeStruct((rows_here, channels), BF16),
            jax.ShapeDtypeStruct((w_head.shape[0], rows_here), F32),
        ),
        in_specs=[smem, vmem, vmem, vmem, vmem] + [anywhere] * 4,
        out_specs=(vmem, vmem),
        scratch_shapes=[
            pltpu.VMEM((rows_here, channels), BF16),
            pltpu.VMEM((rows_here, channels), BF16),
            pltpu.VMEM((patches, PATCH, 2 * channels), BF16),
            pltpu.VMEM((rows_here, channels), BF16),
            pltpu.VMEM((rows_here, channels), F32),
        ]
        + weights,
        compiler_params=params,
        cost_estimate=cost,
        name="second_block",
    )(pattern_second, incoming, dest_all, norm_gains, w_head, w_qkv, w_proj, w_up, w_down)
    return features, normals


def solution(mesh):
    split = P(("grp", "seq"))
    return jax.shard_map(
        shards,
        mesh=mesh,
        in_specs=(split, split, split, split) + (P(),) * 6,
        out_specs=(split, P(None, ("grp", "seq"))),
        check_vma=False,
    )
```

```python
import functools

import jax
import jax.numpy as jnp
from jax import lax
from jax.experimental import pallas as pl
from jax.experimental.pallas import tpu as pltpu
from jax.sharding import PartitionSpec as P

HEADS = 8
PATCH = 64
SLOTS = 8
GROUP_HEADS = 4
BF16 = jnp.bfloat16
F32 = jnp.float32
SIDE = 4
REQUESTS = 2
MESH = pl.DeviceIdType.MESH


def norm(rows, gains):
    values = rows.astype(F32)
    centered = values - jnp.mean(values, axis=-1, keepdims=True)
    spread = jnp.mean(centered * centered, axis=-1, keepdims=True)
    return (centered * lax.rsqrt(spread + 1e-05) * gains).astype(BF16)


def mm(a, b):
    return jnp.dot(a, b, preferred_element_type=F32)


def attend_patch(queries, keys, values):
    width = GROUP_HEADS * PATCH
    lane = lax.broadcasted_iota(jnp.int32, (PATCH, width), 1) // PATCH
    mixed = []
    for part in range(HEADS // GROUP_HEADS):
        cols = slice(part * width, (part + 1) * width)
        q = queries[:, cols]
        spread = jnp.concatenate(
            [jnp.where(lane == head, q, jnp.zeros_like(q)) for head in range(GROUP_HEADS)], axis=0
        )
        scores = lax.dot_general(
            spread, keys[:, cols], (((1,), (1,)), ((), ())), preferred_element_type=F32
        )
        top = jnp.max(scores, axis=-1, keepdims=True)
        weights = jnp.exp((scores - top) * PATCH ** (-0.5))
        total = jnp.sum(weights, axis=-1, keepdims=True)
        out = mm(weights.astype(BF16), values[:, cols]) * (1.0 / total)
        acc = jnp.where(lane == 0, out[:PATCH], 0.0)
        for head in range(1, GROUP_HEADS):
            acc = acc + jnp.where(lane == head, out[head * PATCH : (head + 1) * PATCH], 0.0)
        mixed.append(acc)
    return jnp.concatenate(mixed, axis=1).astype(BF16)


def finish(rows, att_ref, gains, wp_ref, wu_ref, wd_ref, acc_ref, waits):
    waits[0]()
    first = (rows.astype(F32) + mm(att_ref[...], wp_ref[...])).astype(BF16)
    hidden = norm(first, gains)
    acc_ref[...] = first.astype(F32)
    waits[1]()
    waits[2]()
    ff = wu_ref.shape[1]
    step = 512
    for at in range(0, ff, step):
        upper = mm(hidden, wu_ref[:, at : at + step])
        act = (0.5 * upper * (1.0 + lax.erf(upper * 0.7071067811865476))).astype(BF16)
        acc_ref[...] += mm(act, wd_ref[at : at + step, :])
    return acc_ref[...].astype(BF16)


def weight_copies(block, sources, targets, sems):
    return [
        pltpu.make_async_copy(source.at[block], target, sems.at[n])
        for n, (source, target) in enumerate(zip(sources, targets))
    ]


def first_kernel(
    pattern, points_hbm, dest_hbm, gains_hbm, qkv_hbm, proj_hbm, up_hbm, down_hbm,
    incoming, in_places, points, dest, gains, asks, out_places, hx0, hx1, hx2, hx3, hz0, hz1, hz2, hz3, got_x, got_z, pats, send, table, picks,
    chosen, q_ref, att_ref, acc_ref, outgoing, wq, wp, wu, wd, weight_sems,
    pat_sems, step_sems, send_sems, recv_sems, table_sem, ready_plane, ready_all, load_sems, row_sems, place_sems,
):
    grp = lax.axis_index("grp")
    seq = lax.axis_index("seq")
    x, z, c = seq // (2 * SIDE), (seq // 2) % SIDE, seq % 2
    patches, patch, channels = points.shape
    half = channels // 2
    places = 2 * SIDE
    loads = [
        pltpu.make_async_copy(source, target, load_sems.at[n])
        for n, (source, target) in enumerate(((points_hbm, points), (dest_hbm, dest), (gains_hbm, gains)))
    ]
    copies = weight_copies(0, (qkv_hbm, proj_hbm, up_hbm, down_hbm), (wq, wp, wu, wd), weight_sems)
    for copy in loads + copies:
        copy.start()
    lane = lax.broadcasted_iota(jnp.int32, asks.shape, 1)
    asking = jnp.full(asks.shape, -1, jnp.int32)
    named = [pattern[j, p] for p in range(patches) for j in range(pattern.shape[0])]
    for n, name in enumerate(named):
        asking = jnp.where(lane == n, name, asking)
    asks[...] = asking

    def at(axis, step, other):
        core = (c + other) % 2
        if axis == 0:
            place = (x + step) % SIDE
            return (grp, (place * SIDE + z) * 2 + core), place * 2 + core
        place = (z + step) % SIDE
        return (grp, (x * SIDE + place) * 2 + core), place * 2 + core

    def across(step):
        return ((grp + step) % SIDE, seq)

    peers = [(axis, step, other) for axis in (0, 1) for step in range(SIDE) for other in (0, 1)]
    peers = [peer for peer in peers if peer[1:] != (0, 0)]
    steps = (1, SIDE - 1, 2)
    barrier = pltpu.get_barrier_semaphore()
    for peer in peers:
        pl.semaphore_signal(barrier, inc=1, device_id=at(*peer)[0], device_id_type=MESH)
    for step in steps:
        pl.semaphore_signal(barrier, inc=1, device_id=across(step), device_id_type=MESH)
    pl.semaphore_wait(barrier, len(peers) + len(steps))

    along = (x, z)
    mine = (x * 2 + c, z * 2 + c)
    held = ((hx0, hx1, hx2, hx3), (hz0, hz1, hz2, hz3))
    got = (got_x, got_z)

    def first_step(axis, step):
        return pltpu.make_async_remote_copy(
            src_ref=points.at[:, :, pl.ds(axis * half, half)],
            dst_ref=held[axis][SIDE - step],
            send_sem=step_sems.at[axis, 0, step],
            recv_sem=step_sems.at[axis, 1, SIDE - step],
            device_id=at(axis, step, 0)[0],
            device_id_type=MESH,
        )

    def ask(axis, step, other, place):
        return pltpu.make_async_remote_copy(
            src_ref=asks,
            dst_ref=pats.at[axis * places + place],
            send_sem=pat_sems.at[0, axis * places + step * 2 + other],
            recv_sem=pat_sems.at[1, axis * places + place],
            device_id=at(axis, step, other)[0],
            device_id_type=MESH,
        )

    for peer in peers:
        ask(*peer, mine[peer[0]]).start()
    loads[0].wait()
    for step in steps:
        for axis in (0, 1):
            first_step(axis, step).start()
    for step in steps:
        pl.semaphore_signal(ready_plane, inc=1, device_id=at(0, step, 0)[0], device_id_type=MESH)
    for axis in (0, 1):
        held[axis][0][...] = points[:, :, axis * half : (axis + 1) * half]
        pats[axis * places + mine[axis]] = asks[...]
    for peer in peers:
        ask(*peer, at(*peer)[1]).wait()

    asked = pats[...].reshape(2 * places, pats.shape[2])
    lane = lax.broadcasted_iota(jnp.int32, asked.shape, 1)
    in_row = lax.broadcasted_iota(jnp.int32, asked.shape, 0) < places
    found = jnp.zeros_like(asked)
    for k in range(SIDE):
        source = jnp.where(in_row, (x * SIDE + k) * 2 + c, (k * SIDE + z) * 2 + c)
        match = (asked >> 3) == source
        first = jnp.min(jnp.where(match, lane, asked.shape[1]), axis=1, keepdims=True)
        local = asked & 7
        one = jnp.sum(jnp.where(match & (lane == first), local, 0), axis=1, keepdims=True)
        two = jnp.sum(jnp.where(match & (lane != first), local, 0), axis=1, keepdims=True) & 7
        found = jnp.where(lane == 2 * k, one, jnp.where(lane == 2 * k + 1, two, found))
    table[...] = found
    load = pltpu.make_async_copy(table, picks, table_sem)
    load.start()
    load.wait()

    def pass_on(axis, step, other, turn, k, place):
        return pltpu.make_async_remote_copy(
            src_ref=send.at[axis, step * 2 + other, turn],
            dst_ref=got[axis].at[place, k],
            send_sem=send_sems.at[axis, step * 2 + other, turn],
            recv_sem=recv_sems.at[axis, place, k],
            device_id=at(1 - axis, step, other)[0],
            device_id_type=MESH,
        )

    askers = [(step, other) for step in steps + (0,) for other in (0, 1)]
    for turn in (0,) + tuple(SIDE - step for step in steps):
        for axis in (0, 1):
            k = (along[axis] + turn) % SIDE
            if turn:
                first_step(axis, SIDE - turn).wait_recv()
            for step, other in askers:
                row = (1 - axis) * places + at(1 - axis, step, other)[1]
                for r in range(REQUESTS):
                    part = held[axis][turn][picks[row, REQUESTS * k + r]]
                    if (step, other) == (0, 0):
                        got[axis][mine[1 - axis], k, r] = part
                    else:
                        send[axis, step * 2 + other, turn, r] = part
                if (step, other) != (0, 0):
                    pass_on(axis, step, other, turn, k, mine[1 - axis]).start()
    pl.semaphore_wait(ready_plane, len(steps))
    for step in steps:
        pl.semaphore_signal(ready_all, inc=1, device_id=across(step), device_id_type=MESH)

    rows_here = patches * patch
    devices = incoming.shape[0]
    loads[1].wait()
    loads[2].wait()
    target = dest[...] >> 9
    on_device = lax.broadcasted_iota(jnp.int32, (devices, rows_here), 0) == target
    before = lax.broadcasted_iota(jnp.int32, (rows_here, rows_here), 0) < lax.broadcasted_iota(
        jnp.int32, (rows_here, rows_here), 1
    )
    earlier = mm(on_device.astype(BF16), before.astype(BF16))
    rank = jnp.sum(jnp.where(on_device, earlier, 0.0), axis=0, keepdims=True)
    slot = target * SLOTS + rank.astype(jnp.int32)
    lane = lax.broadcasted_iota(jnp.int32, (devices, 128), 1)
    place = (dest[...] & 511) + 1
    table_out = jnp.zeros((devices, 128), jnp.int32)
    for j in range(SLOTS):
        here = jnp.where(on_device & (earlier == j), place, 0)
        table_out = jnp.where(lane == j, jnp.sum(here, axis=1, keepdims=True), table_out)
    out_places[...] = table_out.reshape(devices, 1, 128)

    pl.semaphore_wait(ready_all, len(steps))
    group = devices // SIDE
    me = grp * group + seq

    def send_to(source, target, sems, to):
        return pltpu.make_async_remote_copy(
            src_ref=source.at[to],
            dst_ref=target.at[me],
            send_sem=sems.at[0],
            recv_sem=sems.at[1],
            device_id=(to // group, to % group),
            device_id_type=MESH,
        )

    def arrive(source, target, sems):
        blocks = pl.ds(0, devices - 1)
        pltpu.make_async_remote_copy(
            src_ref=source.at[blocks],
            dst_ref=target.at[blocks],
            send_sem=sems.at[0],
            recv_sem=sems.at[1],
            device_id=across(1),
            device_id_type=MESH,
        ).wait()

    def send_places(k, carry):
        send_to(out_places, in_places, place_sems, (me + k) % devices).start()
        return carry

    lax.fori_loop(1, devices, send_places, 0)
    in_places[me] = out_places[me]
    gain = gains[0:1]
    rows = points[...].reshape(rows_here, channels)
    copies[0].wait()
    q_ref[...] = mm(norm(rows, gain), wq[:, :channels]).astype(BF16)

    for axis in (0, 1):
        for step in steps:
            first_step(axis, step).wait_send()
        for step, other in askers:
            if (step, other) != (0, 0):
                for k in range(SIDE):
                    pass_on(axis, step, other, k, k, at(1 - axis, step, other)[1]).wait()

    owners = []
    for p in range(patches):
        chosen[p, :patch] = points[p]
        for j in range(pattern.shape[0]):
            owner = named[p * pattern.shape[0] + j] >> 3
            r = jnp.int32(0)
            for earlier_owner in owners:
                r = r + jnp.where(earlier_owner == owner, 1, 0)
            owners.append(owner)
            r = jnp.minimum(r, REQUESTS - 1)
            ox, oz, oc = owner // places, (owner // 2) % SIDE, owner % 2
            to = slice((j + 1) * patch, (j + 2) * patch)
            chosen[p, to, :half] = got_x[oz * 2 + oc, ox, r]
            chosen[p, to, half:] = got_z[ox * 2 + oc, oz, r]

    def one(p, carry):
        hidden = norm(chosen[p], gain)
        kv = mm(hidden, wq[:, channels:]).astype(BF16)
        start = pl.multiple_of(p * patch, patch)
        att_ref[pl.ds(start, patch)] = attend_patch(
            q_ref[pl.ds(start, patch)], kv[:, :channels], kv[:, channels:]
        )
        return carry

    lax.fori_loop(0, patches, one, 0)
    done = finish(rows, att_ref, gains[1:2], wp, wu, wd, acc_ref, [copy.wait for copy in copies[1:]])

    for turn in range(SIDE):
        to_grp = (grp + turn) % SIDE
        match = (
            lax.broadcasted_iota(jnp.int32, (group * SLOTS, rows_here), 0) + to_grp * (group * SLOTS) == slot
        )
        outgoing[pl.ds(to_grp * group, group)] = (
            mm(match.astype(BF16), done).astype(BF16).reshape(group, SLOTS, channels)
        )

        def send_rows(k, carry):
            send_to(outgoing, incoming, row_sems, to_grp * group + (seq + k) % group).start()
            return carry

        lax.fori_loop(1 if turn == 0 else 0, group, send_rows, 0)
    incoming[me] = outgoing[me]
    arrive(out_places, in_places, place_sems)
    arrive(outgoing, incoming, row_sems)


def second_kernel(
    pattern, incoming, places, gains_hbm, head_hbm, qkv_hbm, proj_hbm, up_hbm, down_hbm,
    features, normals, gains, head, rows_ref, q_ref, kv_ref, att_ref, acc_ref, wq, wp, wu, wd, sems, load_sems,
):
    loads = [
        pltpu.make_async_copy(source, target, load_sems.at[n])
        for n, (source, target) in enumerate(
            ((gains_hbm, gains), (head_hbm, head))
        )
    ]
    copies = weight_copies(1, (qkv_hbm, proj_hbm, up_hbm, down_hbm), (wq, wp, wu, wd), sems)
    for copy in loads + copies:
        copy.start()
    picks, patches = pattern.shape
    rows_here, channels = features.shape
    devices = places.shape[0]
    slots = devices * SLOTS
    table = jnp.transpose(places[...].reshape(devices, 128))[:SLOTS]
    spread = (
        lax.broadcasted_iota(jnp.int32, (devices, slots), 1) // SLOTS
        == lax.broadcasted_iota(jnp.int32, (devices, slots), 0)
    ).astype(BF16)
    high = mm((table >> 4).astype(F32).astype(BF16), spread)
    low = mm((table & 15).astype(F32).astype(BF16), spread)
    of_rank = (
        lax.broadcasted_iota(jnp.int32, (SLOTS, slots), 1) % SLOTS
        == lax.broadcasted_iota(jnp.int32, (SLOTS, slots), 0)
    )
    slot_place = jnp.sum(
        jnp.where(of_rank, high * 16.0 + low, 0.0), axis=0, keepdims=True
    ).astype(jnp.int32)
    step = 256
    for at in range(0, rows_here, step):
        match = lax.broadcasted_iota(jnp.int32, (step, slots), 0) + (at + 1) == slot_place
        rows_ref[at : at + step] = mm(match.astype(BF16), incoming[...]).astype(BF16)
    loads[0].wait()
    copies[0].wait()
    hidden = norm(rows_ref[...], gains[2:3])
    q_ref[...] = mm(hidden, wq[:, :channels]).astype(BF16)
    kv_ref[...] = (
        mm(hidden, wq[:, channels:]).astype(BF16).reshape(patches, PATCH, 2 * channels)
    )

    def one(p, carry):
        kv = jnp.concatenate([kv_ref[p]] + [kv_ref[pattern[j, p]] for j in range(picks)], axis=0)
        at = pl.multiple_of(p * PATCH, PATCH)
        att_ref[pl.ds(at, PATCH)] = attend_patch(
            q_ref[pl.ds(at, PATCH)], kv[:, :channels], kv[:, channels:]
        )
        return carry

    lax.fori_loop(0, patches, one, 0)
    done = finish(
        rows_ref[...], att_ref, gains[3:4], wp, wu, wd, acc_ref, [copy.wait for copy in copies[1:]]
    )
    features[...] = done
    loads[1].wait()
    normals[...] = lax.dot_general(
        head[...], done, (((1,), (1,)), ((), ())), preferred_element_type=F32
    )


def shards(
    points, pattern_first, pattern_second, destination, norm_gains, w_qkv, w_proj, w_up, w_down, w_head
):
    rows_here, channels = points.shape
    patches = rows_here // PATCH
    ff = w_up.shape[2]
    devices = lax.axis_size("grp") * lax.axis_size("seq")
    slots = devices * SLOTS
    vmem = pl.BlockSpec(memory_space=pltpu.VMEM)
    smem = pl.BlockSpec(memory_space=pltpu.SMEM)
    hbm = pl.BlockSpec(memory_space=pltpu.HBM)
    weights = [
        pltpu.VMEM((channels, 3 * channels), BF16),
        pltpu.VMEM((channels, channels), BF16),
        pltpu.VMEM((channels, ff), BF16),
        pltpu.VMEM((ff, channels), BF16),
        pltpu.SemaphoreType.DMA((4,)),
    ]
    params = pltpu.CompilerParams(vmem_limit_bytes=48 << 20)
    work = 2 * rows_here * channels * (4 * channels + 2 * ff)
    cost = pl.CostEstimate(flops=2 * work, bytes_accessed=8 << 20, transcendentals=rows_here * ff)
    places = 2 * SIDE
    half = channels // 2
    keep = lambda array: pltpu.with_memory_space_constraint(array, pltpu.HBM)
    stacks = [keep(array) for array in (w_qkv, w_proj, w_up, w_down)]
    incoming, places_in = pl.pallas_call(
        first_kernel,
        out_shape=(
            jax.ShapeDtypeStruct((devices, SLOTS, channels), BF16),
            jax.ShapeDtypeStruct((devices, 1, 128), jnp.int32),
        ),
        in_specs=[smem] + [hbm] * 7,
        out_specs=(vmem, vmem),
        scratch_shapes=[
            pltpu.VMEM((patches, PATCH, channels), BF16),
            pltpu.VMEM((1, rows_here), jnp.int32),
            pltpu.VMEM(norm_gains.shape, F32),
            pltpu.VMEM((1, 128), jnp.int32),
            pltpu.VMEM((devices, 1, 128), jnp.int32),
        ]
        + [pltpu.VMEM((patches, PATCH, half), BF16)] * (2 * SIDE)
        + [pltpu.VMEM((places, SIDE, REQUESTS, PATCH, half), BF16)] * 2
        + [
            pltpu.VMEM((2 * places, 1, 128), jnp.int32),
            pltpu.VMEM((2, places, SIDE, REQUESTS, PATCH, half), BF16),
            pltpu.VMEM((2 * places, 128), jnp.int32),
            pltpu.SMEM((2 * places, 128), jnp.int32),
            pltpu.VMEM((patches, 4 * PATCH, channels), BF16),
            pltpu.VMEM((rows_here, channels), BF16),
            pltpu.VMEM((rows_here, channels), BF16),
            pltpu.VMEM((rows_here, channels), F32),
            pltpu.VMEM((devices, SLOTS, channels), BF16),
        ]
        + weights
        + [
            pltpu.SemaphoreType.DMA((2, 2 * places)),
            pltpu.SemaphoreType.DMA((2, 2, SIDE)),
            pltpu.SemaphoreType.DMA((2, places, SIDE)),
            pltpu.SemaphoreType.DMA((2, places, SIDE)),
            pltpu.SemaphoreType.DMA,
            pltpu.SemaphoreType.REGULAR,
            pltpu.SemaphoreType.REGULAR,
            pltpu.SemaphoreType.DMA((3,)),
            pltpu.SemaphoreType.DMA((2,)),
            pltpu.SemaphoreType.DMA((2,)),
        ],
        compiler_params=pltpu.CompilerParams(
            vmem_limit_bytes=48 << 20, collective_id=0, has_side_effects=True
        ),
        cost_estimate=cost,
        name="first_block",
    )(
        pattern_first.T,
        keep(points.reshape(patches, PATCH, channels)),
        keep(destination.reshape(1, rows_here)),
        keep(norm_gains),
        *stacks,
    )
    features, normals = pl.pallas_call(
        second_kernel,
        out_shape=(
            jax.ShapeDtypeStruct((rows_here, channels), BF16),
            jax.ShapeDtypeStruct((w_head.shape[0], rows_here), F32),
        ),
        in_specs=[smem, vmem, vmem] + [hbm] * 6,
        out_specs=(vmem, vmem),
        scratch_shapes=[
            pltpu.VMEM(norm_gains.shape, F32),
            pltpu.VMEM(w_head.shape, BF16),
            pltpu.VMEM((rows_here, channels), BF16),
            pltpu.VMEM((rows_here, channels), BF16),
            pltpu.VMEM((patches, PATCH, 2 * channels), BF16),
            pltpu.VMEM((rows_here, channels), BF16),
            pltpu.VMEM((rows_here, channels), F32),
        ]
        + weights
        + [pltpu.SemaphoreType.DMA((2,))],
        compiler_params=params,
        cost_estimate=cost,
        name="second_block",
    )(
        pattern_second.T,
        incoming.reshape(slots, channels),
        places_in,
        keep(norm_gains),
        keep(w_head),
        *stacks,
    )
    return features, normals


def solution(mesh):
    split = P(("grp", "seq"))
    return jax.shard_map(
        shards,
        mesh=mesh,
        in_specs=(split, split, split, split) + (P(),) * 6,
        out_specs=(split, P(None, ("grp", "seq"))),
        check_vma=False,
    )
```

```python
import functools

import jax
import jax.numpy as jnp
from jax import lax
from jax.experimental import pallas as pl
from jax.experimental.pallas import tpu as pltpu
from jax.sharding import PartitionSpec as P

HEADS = 8
PATCH = 64
SLOTS = 8
GROUP_HEADS = 4
BF16 = jnp.bfloat16
F32 = jnp.float32
SIDE = 4
REQUESTS = 2
MESH = pl.DeviceIdType.MESH


def norm(rows, gains):
    values = rows.astype(F32)
    centered = values - jnp.mean(values, axis=-1, keepdims=True)
    spread = jnp.mean(centered * centered, axis=-1, keepdims=True)
    return (centered * lax.rsqrt(spread + 1e-05) * gains).astype(BF16)


def mm(a, b):
    return jnp.dot(a, b, preferred_element_type=F32)


def attend_patch(queries, keys, values):
    width = GROUP_HEADS * PATCH
    lane = lax.broadcasted_iota(jnp.int32, (PATCH, width), 1) // PATCH
    mixed = []
    for part in range(HEADS // GROUP_HEADS):
        cols = slice(part * width, (part + 1) * width)
        q = queries[:, cols]
        spread = jnp.concatenate(
            [jnp.where(lane == head, q, jnp.zeros_like(q)) for head in range(GROUP_HEADS)], axis=0
        )
        scores = lax.dot_general(
            spread, keys[:, cols], (((1,), (1,)), ((), ())), preferred_element_type=F32
        )
        top = jnp.max(scores, axis=-1, keepdims=True)
        weights = jnp.exp((scores - top) * PATCH ** (-0.5))
        total = jnp.sum(weights, axis=-1, keepdims=True)
        out = mm(weights.astype(BF16), values[:, cols]) * (1.0 / total)
        acc = jnp.where(lane == 0, out[:PATCH], 0.0)
        for head in range(1, GROUP_HEADS):
            acc = acc + jnp.where(lane == head, out[head * PATCH : (head + 1) * PATCH], 0.0)
        mixed.append(acc)
    return jnp.concatenate(mixed, axis=1).astype(BF16)


def finish(rows, att_ref, gains, wp_ref, wu_ref, wd_ref, acc_ref, waits):
    waits[0]()
    first = (rows.astype(F32) + mm(att_ref[...], wp_ref[...])).astype(BF16)
    hidden = norm(first, gains)
    acc_ref[...] = first.astype(F32)
    waits[1]()
    waits[2]()
    ff = wu_ref.shape[1]
    step = 512
    for at in range(0, ff, step):
        upper = mm(hidden, wu_ref[:, at : at + step])
        act = (0.5 * upper * (1.0 + lax.erf(upper * 0.7071067811865476))).astype(BF16)
        acc_ref[...] += mm(act, wd_ref[at : at + step, :])
    return acc_ref[...].astype(BF16)


def weight_copies(block, sources, targets, sems):
    return [
        pltpu.make_async_copy(source.at[block], target, sems.at[n])
        for n, (source, target) in enumerate(zip(sources, targets))
    ]


def first_kernel(
    pattern, points_hbm, dest_hbm, gains_hbm, qkv_hbm, proj_hbm, up_hbm, down_hbm,
    incoming, in_places, points, dest, gains, asks, out_places, hx0, hx1, hx2, hx3, hz0, hz1, hz2, hz3, got_x, got_z, pats, send, table, picks,
    chosen, q_ref, kv_ref, att_ref, acc_ref, outgoing, wq, wp, wu, wd, weight_sems,
    pat_sems, step_sems, send_sems, recv_sems, table_sem, ready_plane, ready_all, load_sems, row_sems, place_sems,
):
    grp = lax.axis_index("grp")
    seq = lax.axis_index("seq")
    x, z, c = seq // (2 * SIDE), (seq // 2) % SIDE, seq % 2
    patches, patch, channels = points.shape
    half = channels // 2
    places = 2 * SIDE
    loads = [
        pltpu.make_async_copy(source, target, load_sems.at[n])
        for n, (source, target) in enumerate(((points_hbm, points), (dest_hbm, dest), (gains_hbm, gains)))
    ]
    copies = weight_copies(0, (qkv_hbm, proj_hbm, up_hbm, down_hbm), (wq, wp, wu, wd), weight_sems)
    for copy in loads + copies:
        copy.start()
    lane = lax.broadcasted_iota(jnp.int32, asks.shape, 1)
    asking = jnp.full(asks.shape, -1, jnp.int32)
    named = [pattern[j, p] for p in range(patches) for j in range(pattern.shape[0])]
    for n, name in enumerate(named):
        asking = jnp.where(lane == n, name, asking)
    asks[...] = asking

    def at(axis, step, other):
        core = (c + other) % 2
        if axis == 0:
            place = (x + step) % SIDE
            return (grp, (place * SIDE + z) * 2 + core), place * 2 + core
        place = (z + step) % SIDE
        return (grp, (x * SIDE + place) * 2 + core), place * 2 + core

    def across(step):
        return ((grp + step) % SIDE, seq)

    peers = [(axis, step, other) for axis in (0, 1) for step in range(SIDE) for other in (0, 1)]
    peers = [peer for peer in peers if peer[1:] != (0, 0)]
    steps = (1, SIDE - 1, 2)
    barrier = pltpu.get_barrier_semaphore()
    for peer in peers:
        pl.semaphore_signal(barrier, inc=1, device_id=at(*peer)[0], device_id_type=MESH)
    for step in steps:
        pl.semaphore_signal(barrier, inc=1, device_id=across(step), device_id_type=MESH)
    pl.semaphore_wait(barrier, len(peers) + len(steps))

    along = (x, z)
    mine = (x * 2 + c, z * 2 + c)
    held = ((hx0, hx1, hx2, hx3), (hz0, hz1, hz2, hz3))
    got = (got_x, got_z)

    def half_rows(part):
        return pl.ds(part * (patches // 2), patches // 2)

    def first_step(axis, step, part):
        return pltpu.make_async_remote_copy(
            src_ref=points.at[half_rows(part), :, pl.ds(axis * half, half)],
            dst_ref=held[axis][SIDE - step].at[half_rows(part)],
            send_sem=step_sems.at[axis, 0, step, part],
            recv_sem=step_sems.at[axis, 1, SIDE - step, part],
            device_id=at(axis, step, 0)[0],
            device_id_type=MESH,
        )

    def relay(axis, part):
        turn, step = ((SIDE - 1, 1), (1, SIDE - 1))[part]
        return pltpu.make_async_remote_copy(
            src_ref=held[axis][turn].at[half_rows(part)],
            dst_ref=held[axis][2].at[half_rows(part)],
            send_sem=step_sems.at[axis, 0, 2, part],
            recv_sem=step_sems.at[axis, 1, 2, part],
            device_id=at(axis, step, 0)[0],
            device_id_type=MESH,
        )

    def ask(axis, step, other, place):
        return pltpu.make_async_remote_copy(
            src_ref=asks,
            dst_ref=pats.at[axis * places + place],
            send_sem=pat_sems.at[0, axis * places + step * 2 + other],
            recv_sem=pat_sems.at[1, axis * places + place],
            device_id=at(axis, step, other)[0],
            device_id_type=MESH,
        )

    for peer in peers:
        ask(*peer, mine[peer[0]]).start()
    loads[0].wait()
    for early in (0, 1):
        for axis in (0, 1):
            first_step(axis, 1, early).start()
            first_step(axis, SIDE - 1, 1 - early).start()
    for step in steps:
        pl.semaphore_signal(ready_plane, inc=1, device_id=at(0, step, 0)[0], device_id_type=MESH)
    for axis in (0, 1):
        held[axis][0][...] = points[:, :, axis * half : (axis + 1) * half]
        pats[axis * places + mine[axis]] = asks[...]
    for peer in peers:
        ask(*peer, at(*peer)[1]).wait()

    asked = pats[...].reshape(2 * places, pats.shape[2])
    lane = lax.broadcasted_iota(jnp.int32, asked.shape, 1)
    in_row = lax.broadcasted_iota(jnp.int32, asked.shape, 0) < places
    found = jnp.zeros_like(asked)
    for k in range(SIDE):
        source = jnp.where(in_row, (x * SIDE + k) * 2 + c, (k * SIDE + z) * 2 + c)
        match = (asked >> 3) == source
        first = jnp.min(jnp.where(match, lane, asked.shape[1]), axis=1, keepdims=True)
        local = asked & 7
        one = jnp.sum(jnp.where(match & (lane == first), local, 0), axis=1, keepdims=True)
        two = jnp.sum(jnp.where(match & (lane != first), local, 0), axis=1, keepdims=True) & 7
        found = jnp.where(lane == 2 * k, one, jnp.where(lane == 2 * k + 1, two, found))
    table[...] = found
    load = pltpu.make_async_copy(table, picks, table_sem)
    load.start()
    load.wait()
    for axis in (0, 1):
        for part in (0, 1):
            first_step(axis, (1, SIDE - 1)[part], part).wait_recv()
            relay(axis, part).start()

    def pass_on(axis, step, other, turn, k, place):
        return pltpu.make_async_remote_copy(
            src_ref=send.at[axis, step * 2 + other, turn],
            dst_ref=got[axis].at[place, k],
            send_sem=send_sems.at[axis, step * 2 + other, turn],
            recv_sem=recv_sems.at[axis, place, k],
            device_id=at(1 - axis, step, other)[0],
            device_id_type=MESH,
        )

    askers = [(step, other) for step in steps + (0,) for other in (0, 1)]
    for turn in (0,) + tuple(SIDE - step for step in steps):
        for axis in (0, 1):
            k = (along[axis] + turn) % SIDE
            if turn == 2:
                for part in (0, 1):
                    relay(axis, part).wait_recv()
            elif turn:
                first_step(axis, SIDE - turn, int(turn == SIDE - 1)).wait_recv()
            for step, other in askers:
                row = (1 - axis) * places + at(1 - axis, step, other)[1]
                for r in range(REQUESTS):
                    part = held[axis][turn][picks[row, REQUESTS * k + r]]
                    if (step, other) == (0, 0):
                        got[axis][mine[1 - axis], k, r] = part
                    else:
                        send[axis, step * 2 + other, turn, r] = part
                if (step, other) != (0, 0):
                    pass_on(axis, step, other, turn, k, mine[1 - axis]).start()
    pl.semaphore_wait(ready_plane, len(steps))
    for step in steps:
        pl.semaphore_signal(ready_all, inc=1, device_id=across(step), device_id_type=MESH)

    rows_here = patches * patch
    devices = incoming.shape[0]
    loads[1].wait()
    loads[2].wait()
    target = dest[...] >> 9
    on_device = lax.broadcasted_iota(jnp.int32, (devices, rows_here), 0) == target
    before = lax.broadcasted_iota(jnp.int32, (rows_here, rows_here), 0) < lax.broadcasted_iota(
        jnp.int32, (rows_here, rows_here), 1
    )
    earlier = mm(on_device.astype(BF16), before.astype(BF16))
    rank = jnp.sum(jnp.where(on_device, earlier, 0.0), axis=0, keepdims=True)
    slot = target * SLOTS + rank.astype(jnp.int32)
    lane = lax.broadcasted_iota(jnp.int32, (devices, 128), 1)
    place = (dest[...] & 511) + 1
    table_out = jnp.zeros((devices, 128), jnp.int32)
    for j in range(SLOTS):
        here = jnp.where(on_device & (earlier == j), place, 0)
        table_out = jnp.where(lane == j, jnp.sum(here, axis=1, keepdims=True), table_out)
    out_places[...] = table_out.reshape(devices, 1, 128)

    pl.semaphore_wait(ready_all, len(steps))
    group = devices // SIDE
    me = grp * group + seq

    def send_to(source, target, sems, to):
        return pltpu.make_async_remote_copy(
            src_ref=source.at[to],
            dst_ref=target.at[me],
            send_sem=sems.at[0],
            recv_sem=sems.at[1],
            device_id=(to // group, to % group),
            device_id_type=MESH,
        )

    def arrive(source, target, sems):
        blocks = pl.ds(0, devices - 1)
        pltpu.make_async_remote_copy(
            src_ref=source.at[blocks],
            dst_ref=target.at[blocks],
            send_sem=sems.at[0],
            recv_sem=sems.at[1],
            device_id=across(1),
            device_id_type=MESH,
        ).wait()

    def send_places(k, carry):
        send_to(out_places, in_places, place_sems, (me + k) % devices).start()
        return carry

    lax.fori_loop(1, devices, send_places, 0)
    in_places[me] = out_places[me]
    gain = gains[0:1]
    rows = points[...].reshape(rows_here, channels)
    copies[0].wait()
    hidden = norm(rows, gain)
    q_ref[...] = mm(hidden, wq[:, :channels]).astype(BF16)
    kv_ref[...] = mm(hidden, wq[:, channels:]).astype(BF16).reshape(patches, patch, 2 * channels)

    for axis in (0, 1):
        for part in (0, 1):
            first_step(axis, 1, part).wait_send()
            first_step(axis, SIDE - 1, part).wait_send()
            relay(axis, part).wait_send()
        for step, other in askers:
            if (step, other) != (0, 0):
                for k in range(SIDE):
                    pass_on(axis, step, other, k, k, at(1 - axis, step, other)[1]).wait()

    owners = []
    for p in range(patches):
        for j in range(pattern.shape[0]):
            owner = named[p * pattern.shape[0] + j] >> 3
            r = jnp.int32(0)
            for earlier_owner in owners:
                r = r + jnp.where(earlier_owner == owner, 1, 0)
            owners.append(owner)
            r = jnp.minimum(r, REQUESTS - 1)
            ox, oz, oc = owner // places, (owner // 2) % SIDE, owner % 2
            to = slice(j * patch, (j + 1) * patch)
            chosen[p, to, :half] = got_x[oz * 2 + oc, ox, r]
            chosen[p, to, half:] = got_z[ox * 2 + oc, oz, r]

    def one(p, carry):
        hidden = norm(chosen[p], gain)
        kv = jnp.concatenate([kv_ref[p], mm(hidden, wq[:, channels:]).astype(BF16)], axis=0)
        start = pl.multiple_of(p * patch, patch)
        att_ref[pl.ds(start, patch)] = attend_patch(
            q_ref[pl.ds(start, patch)], kv[:, :channels], kv[:, channels:]
        )
        return carry

    lax.fori_loop(0, patches, one, 0, unroll=True)
    done = finish(rows, att_ref, gains[1:2], wp, wu, wd, acc_ref, [copy.wait for copy in copies[1:]])

    for turn in range(SIDE):
        to_grp = (grp + turn) % SIDE
        match = (
            lax.broadcasted_iota(jnp.int32, (group * SLOTS, rows_here), 0) + to_grp * (group * SLOTS) == slot
        )
        outgoing[pl.ds(to_grp * group, group)] = (
            mm(match.astype(BF16), done).astype(BF16).reshape(group, SLOTS, channels)
        )

        def send_rows(k, carry):
            send_to(outgoing, incoming, row_sems, to_grp * group + (seq + k) % group).start()
            return carry

        lax.fori_loop(1 if turn == 0 else 0, group, send_rows, 0)
    incoming[me] = outgoing[me]
    arrive(out_places, in_places, place_sems)
    arrive(outgoing, incoming, row_sems)


def second_kernel(
    pattern, incoming, places, gains_hbm, head_hbm, qkv_hbm, proj_hbm, up_hbm, down_hbm,
    features, normals, gains, head, rows_ref, q_ref, kv_ref, att_ref, acc_ref, wq, wp, wu, wd, sems, load_sems,
):
    loads = [
        pltpu.make_async_copy(source, target, load_sems.at[n])
        for n, (source, target) in enumerate(
            ((gains_hbm, gains), (head_hbm, head))
        )
    ]
    copies = weight_copies(1, (qkv_hbm, proj_hbm, up_hbm, down_hbm), (wq, wp, wu, wd), sems)
    for copy in loads + copies:
        copy.start()
    picks, patches = pattern.shape
    rows_here, channels = features.shape
    devices = places.shape[0]
    slots = devices * SLOTS
    table = jnp.transpose(places[...].reshape(devices, 128))[:SLOTS]
    spread = (
        lax.broadcasted_iota(jnp.int32, (devices, slots), 1) // SLOTS
        == lax.broadcasted_iota(jnp.int32, (devices, slots), 0)
    ).astype(BF16)
    high = mm((table >> 4).astype(F32).astype(BF16), spread)
    low = mm((table & 15).astype(F32).astype(BF16), spread)
    of_rank = (
        lax.broadcasted_iota(jnp.int32, (SLOTS, slots), 1) % SLOTS
        == lax.broadcasted_iota(jnp.int32, (SLOTS, slots), 0)
    )
    slot_place = jnp.sum(
        jnp.where(of_rank, high * 16.0 + low, 0.0), axis=0, keepdims=True
    ).astype(jnp.int32)
    step = 256
    for at in range(0, rows_here, step):
        match = lax.broadcasted_iota(jnp.int32, (step, slots), 0) + (at + 1) == slot_place
        rows_ref[at : at + step] = mm(match.astype(BF16), incoming[...]).astype(BF16)
    loads[0].wait()
    copies[0].wait()
    hidden = norm(rows_ref[...], gains[2:3])
    q_ref[...] = mm(hidden, wq[:, :channels]).astype(BF16)
    kv_ref[...] = (
        mm(hidden, wq[:, channels:]).astype(BF16).reshape(patches, PATCH, 2 * channels)
    )

    def one(p, carry):
        kv = jnp.concatenate([kv_ref[p]] + [kv_ref[pattern[j, p]] for j in range(picks)], axis=0)
        at = pl.multiple_of(p * PATCH, PATCH)
        att_ref[pl.ds(at, PATCH)] = attend_patch(
            q_ref[pl.ds(at, PATCH)], kv[:, :channels], kv[:, channels:]
        )
        return carry

    lax.fori_loop(0, patches, one, 0, unroll=True)
    done = finish(
        rows_ref[...], att_ref, gains[3:4], wp, wu, wd, acc_ref, [copy.wait for copy in copies[1:]]
    )
    features[...] = done
    loads[1].wait()
    normals[...] = lax.dot_general(
        head[...], done, (((1,), (1,)), ((), ())), preferred_element_type=F32
    )


def shards(
    points, pattern_first, pattern_second, destination, norm_gains, w_qkv, w_proj, w_up, w_down, w_head
):
    rows_here, channels = points.shape
    patches = rows_here // PATCH
    ff = w_up.shape[2]
    devices = lax.axis_size("grp") * lax.axis_size("seq")
    slots = devices * SLOTS
    vmem = pl.BlockSpec(memory_space=pltpu.VMEM)
    smem = pl.BlockSpec(memory_space=pltpu.SMEM)
    hbm = pl.BlockSpec(memory_space=pltpu.HBM)
    weights = [
        pltpu.VMEM((channels, 3 * channels), BF16),
        pltpu.VMEM((channels, channels), BF16),
        pltpu.VMEM((channels, ff), BF16),
        pltpu.VMEM((ff, channels), BF16),
        pltpu.SemaphoreType.DMA((4,)),
    ]
    params = pltpu.CompilerParams(vmem_limit_bytes=48 << 20)
    work = 2 * rows_here * channels * (4 * channels + 2 * ff)
    cost = pl.CostEstimate(flops=2 * work, bytes_accessed=8 << 20, transcendentals=rows_here * ff)
    places = 2 * SIDE
    half = channels // 2
    keep = lambda array: pltpu.with_memory_space_constraint(array, pltpu.HBM)
    stacks = [keep(array) for array in (w_qkv, w_proj, w_up, w_down)]
    incoming, places_in = pl.pallas_call(
        first_kernel,
        out_shape=(
            jax.ShapeDtypeStruct((devices, SLOTS, channels), BF16),
            jax.ShapeDtypeStruct((devices, 1, 128), jnp.int32),
        ),
        in_specs=[smem] + [hbm] * 7,
        out_specs=(vmem, vmem),
        scratch_shapes=[
            pltpu.VMEM((patches, PATCH, channels), BF16),
            pltpu.VMEM((1, rows_here), jnp.int32),
            pltpu.VMEM(norm_gains.shape, F32),
            pltpu.VMEM((1, 128), jnp.int32),
            pltpu.VMEM((devices, 1, 128), jnp.int32),
        ]
        + [pltpu.VMEM((patches, PATCH, half), BF16)] * (2 * SIDE)
        + [pltpu.VMEM((places, SIDE, REQUESTS, PATCH, half), BF16)] * 2
        + [
            pltpu.VMEM((2 * places, 1, 128), jnp.int32),
            pltpu.VMEM((2, places, SIDE, REQUESTS, PATCH, half), BF16),
            pltpu.VMEM((2 * places, 128), jnp.int32),
            pltpu.SMEM((2 * places, 128), jnp.int32),
            pltpu.VMEM((patches, pattern_first.shape[1] * PATCH, channels), BF16),
            pltpu.VMEM((rows_here, channels), BF16),
            pltpu.VMEM((patches, PATCH, 2 * channels), BF16),
            pltpu.VMEM((rows_here, channels), BF16),
            pltpu.VMEM((rows_here, channels), F32),
            pltpu.VMEM((devices, SLOTS, channels), BF16),
        ]
        + weights
        + [
            pltpu.SemaphoreType.DMA((2, 2 * places)),
            pltpu.SemaphoreType.DMA((2, 2, SIDE, 2)),
            pltpu.SemaphoreType.DMA((2, places, SIDE)),
            pltpu.SemaphoreType.DMA((2, places, SIDE)),
            pltpu.SemaphoreType.DMA,
            pltpu.SemaphoreType.REGULAR,
            pltpu.SemaphoreType.REGULAR,
            pltpu.SemaphoreType.DMA((3,)),
            pltpu.SemaphoreType.DMA((2,)),
            pltpu.SemaphoreType.DMA((2,)),
        ],
        compiler_params=pltpu.CompilerParams(
            vmem_limit_bytes=48 << 20, collective_id=0, has_side_effects=True
        ),
        cost_estimate=cost,
        name="first_block",
    )(
        pattern_first.T,
        keep(points.reshape(patches, PATCH, channels)),
        keep(destination.reshape(1, rows_here)),
        keep(norm_gains),
        *stacks,
    )
    features, normals = pl.pallas_call(
        second_kernel,
        out_shape=(
            jax.ShapeDtypeStruct((rows_here, channels), BF16),
            jax.ShapeDtypeStruct((w_head.shape[0], rows_here), F32),
        ),
        in_specs=[smem, vmem, vmem] + [hbm] * 6,
        out_specs=(vmem, vmem),
        scratch_shapes=[
            pltpu.VMEM(norm_gains.shape, F32),
            pltpu.VMEM(w_head.shape, BF16),
            pltpu.VMEM((rows_here, channels), BF16),
            pltpu.VMEM((rows_here, channels), BF16),
            pltpu.VMEM((patches, PATCH, 2 * channels), BF16),
            pltpu.VMEM((rows_here, channels), BF16),
            pltpu.VMEM((rows_here, channels), F32),
        ]
        + weights
        + [pltpu.SemaphoreType.DMA((2,))],
        compiler_params=params,
        cost_estimate=cost,
        name="second_block",
    )(
        pattern_second.T,
        incoming.reshape(slots, channels),
        places_in,
        keep(norm_gains),
        keep(w_head),
        *stacks,
    )
    return features, normals


def solution(mesh):
    split = P(("grp", "seq"))
    return jax.shard_map(
        shards,
        mesh=mesh,
        in_specs=(split, split, split, split) + (P(),) * 6,
        out_specs=(split, P(None, ("grp", "seq"))),
        check_vma=False,
    )
```

```python
import functools

import jax
import jax.numpy as jnp
from jax import lax
from jax.experimental import pallas as pl
from jax.experimental.pallas import tpu as pltpu
from jax.sharding import PartitionSpec as P

HEADS = 8
PATCH = 64
SLOTS = 8
GROUP_HEADS = 4
BF16 = jnp.bfloat16
F32 = jnp.float32
SIDE = 4
REQUESTS = 2
MESH = pl.DeviceIdType.MESH


def norm(rows, gains):
    values = rows.astype(F32)
    centered = values - jnp.mean(values, axis=-1, keepdims=True)
    spread = jnp.mean(centered * centered, axis=-1, keepdims=True)
    return (centered * lax.rsqrt(spread + 1e-05) * gains).astype(BF16)


def mm(a, b):
    return jnp.dot(a, b, preferred_element_type=F32)


def attend_patch(queries, keys, values):
    width = GROUP_HEADS * PATCH
    lane = lax.broadcasted_iota(jnp.int32, (PATCH, width), 1) // PATCH
    mixed = []
    for part in range(HEADS // GROUP_HEADS):
        cols = slice(part * width, (part + 1) * width)
        q = queries[:, cols]
        spread = jnp.concatenate(
            [jnp.where(lane == head, q, jnp.zeros_like(q)) for head in range(GROUP_HEADS)], axis=0
        )
        scores = lax.dot_general(
            spread, keys[:, cols], (((1,), (1,)), ((), ())), preferred_element_type=F32
        )
        top = jnp.max(scores, axis=-1, keepdims=True)
        weights = jnp.exp((scores - top) * PATCH ** (-0.5))
        total = jnp.sum(weights, axis=-1, keepdims=True)
        out = mm(weights.astype(BF16), values[:, cols]) * (1.0 / total)
        acc = jnp.where(lane == 0, out[:PATCH], 0.0)
        for head in range(1, GROUP_HEADS):
            acc = acc + jnp.where(lane == head, out[head * PATCH : (head + 1) * PATCH], 0.0)
        mixed.append(acc)
    return jnp.concatenate(mixed, axis=1).astype(BF16)


def finish(rows, att_ref, gains, wp_ref, wu_ref, wd_ref, acc_ref, waits):
    waits[0]()
    first = (rows.astype(F32) + mm(att_ref[...], wp_ref[...])).astype(BF16)
    hidden = norm(first, gains)
    acc_ref[...] = first.astype(F32)
    waits[1]()
    waits[2]()
    ff = wu_ref.shape[1]
    step = 512
    for at in range(0, ff, step):
        upper = mm(hidden, wu_ref[:, at : at + step])
        act = (0.5 * upper * (1.0 + lax.erf(upper * 0.7071067811865476))).astype(BF16)
        acc_ref[...] += mm(act, wd_ref[at : at + step, :])
    return acc_ref[...].astype(BF16)


def weight_copies(block, sources, targets, sems):
    return [
        pltpu.make_async_copy(source.at[block], target, sems.at[n])
        for n, (source, target) in enumerate(zip(sources, targets))
    ]


def places_by_slot(places):
    devices = places.shape[0]
    slots = devices * SLOTS
    table = jnp.transpose(places)[:SLOTS]
    spread = (
        lax.broadcasted_iota(jnp.int32, (devices, slots), 1) // SLOTS
        == lax.broadcasted_iota(jnp.int32, (devices, slots), 0)
    ).astype(BF16)
    high = mm((table >> 4).astype(F32).astype(BF16), spread)
    low = mm((table & 15).astype(F32).astype(BF16), spread)
    of_rank = (
        lax.broadcasted_iota(jnp.int32, (SLOTS, slots), 1) % SLOTS
        == lax.broadcasted_iota(jnp.int32, (SLOTS, slots), 0)
    )
    return jnp.sum(
        jnp.where(of_rank, high * 16.0 + low, 0.0), axis=0, keepdims=True
    ).astype(jnp.int32)


def first_kernel(
    pattern_hbm, points_hbm, dest_hbm, gains_hbm, qkv_hbm, proj_hbm, up_hbm, down_hbm,
    incoming, recv_match, pattern, points, dest, gains, asks, out_places, in_places, send_match, hx0, hx1, hx2, hx3, hz0, hz1, hz2, hz3, got_x, got_z, pats, send, table, picks,
    chosen, q_ref, kv_ref, att_ref, acc_ref, outgoing, wq, wp, wu, wd, weight_sems,
    pat_sems, step_sems, send_sems, recv_sems, table_sem, ready_plane, ready_all, load_sems, row_sems, place_sems,
):
    grp = lax.axis_index("grp")
    seq = lax.axis_index("seq")
    x, z, c = seq // (2 * SIDE), (seq // 2) % SIDE, seq % 2
    patches, patch, channels = points.shape
    half = channels // 2
    places = 2 * SIDE
    loads = [
        pltpu.make_async_copy(source, target, load_sems.at[n])
        for n, (source, target) in enumerate(
            ((pattern_hbm, pattern), (points_hbm, points), (dest_hbm, dest), (gains_hbm, gains))
        )
    ]
    copies = weight_copies(0, (qkv_hbm, proj_hbm, up_hbm, down_hbm), (wq, wp, wu, wd), weight_sems)
    for copy in loads + copies:
        copy.start()

    def at(axis, step, other):
        core = (c + other) % 2
        if axis == 0:
            place = (x + step) % SIDE
            return (grp, (place * SIDE + z) * 2 + core), place * 2 + core
        place = (z + step) % SIDE
        return (grp, (x * SIDE + place) * 2 + core), place * 2 + core

    def across(step):
        return ((grp + step) % SIDE, seq)

    peers = [(axis, step, other) for axis in (0, 1) for step in range(SIDE) for other in (0, 1)]
    peers = [peer for peer in peers if peer[1:] != (0, 0)]
    steps = (1, SIDE - 1, 2)
    barrier = pltpu.get_barrier_semaphore()
    for peer in peers:
        pl.semaphore_signal(barrier, inc=1, device_id=at(*peer)[0], device_id_type=MESH)
    for step in steps:
        pl.semaphore_signal(barrier, inc=1, device_id=across(step), device_id_type=MESH)
    loads[0].wait()
    lane = lax.broadcasted_iota(jnp.int32, asks.shape, 1)
    asking = jnp.full(asks.shape, -1, jnp.int32)
    named = [pattern[j, p] for p in range(patches) for j in range(pattern.shape[0])]
    for n, name in enumerate(named):
        asking = jnp.where(lane == n, name, asking)
    asks[...] = asking
    pl.semaphore_wait(barrier, len(peers) + len(steps))

    along = (x, z)
    mine = (x * 2 + c, z * 2 + c)
    held = ((hx0, hx1, hx2, hx3), (hz0, hz1, hz2, hz3))
    got = (got_x, got_z)

    def half_rows(part):
        return pl.ds(part * (patches // 2), patches // 2)

    def first_step(axis, step, part):
        return pltpu.make_async_remote_copy(
            src_ref=points.at[half_rows(part), :, pl.ds(axis * half, half)],
            dst_ref=held[axis][SIDE - step].at[half_rows(part)],
            send_sem=step_sems.at[axis, 0, step, part],
            recv_sem=step_sems.at[axis, 1, SIDE - step, part],
            device_id=at(axis, step, 0)[0],
            device_id_type=MESH,
        )

    def relay(axis, part):
        turn, step = ((SIDE - 1, 1), (1, SIDE - 1))[part]
        return pltpu.make_async_remote_copy(
            src_ref=held[axis][turn].at[half_rows(part)],
            dst_ref=held[axis][2].at[half_rows(part)],
            send_sem=step_sems.at[axis, 0, 2, part],
            recv_sem=step_sems.at[axis, 1, 2, part],
            device_id=at(axis, step, 0)[0],
            device_id_type=MESH,
        )

    def ask(axis, step, other, place):
        return pltpu.make_async_remote_copy(
            src_ref=asks,
            dst_ref=pats.at[axis * places + place],
            send_sem=pat_sems.at[0, axis * places + step * 2 + other],
            recv_sem=pat_sems.at[1, axis * places + place],
            device_id=at(axis, step, other)[0],
            device_id_type=MESH,
        )

    for peer in peers:
        ask(*peer, mine[peer[0]]).start()
    loads[1].wait()
    for early in (0, 1):
        for axis in (0, 1):
            first_step(axis, 1, early).start()
            first_step(axis, SIDE - 1, 1 - early).start()
    for step in steps:
        pl.semaphore_signal(ready_plane, inc=1, device_id=at(0, step, 0)[0], device_id_type=MESH)
    for axis in (0, 1):
        held[axis][0][...] = points[:, :, axis * half : (axis + 1) * half]
        pats[axis * places + mine[axis]] = asks[...]
    for peer in peers:
        ask(*peer, at(*peer)[1]).wait()

    asked = pats[...].reshape(2 * places, pats.shape[2])
    lane = lax.broadcasted_iota(jnp.int32, asked.shape, 1)
    in_row = lax.broadcasted_iota(jnp.int32, asked.shape, 0) < places
    found = jnp.zeros_like(asked)
    for k in range(SIDE):
        source = jnp.where(in_row, (x * SIDE + k) * 2 + c, (k * SIDE + z) * 2 + c)
        match = (asked >> 3) == source
        first = jnp.min(jnp.where(match, lane, asked.shape[1]), axis=1, keepdims=True)
        local = asked & 7
        one = jnp.sum(jnp.where(match & (lane == first), local, 0), axis=1, keepdims=True)
        two = jnp.sum(jnp.where(match & (lane != first), local, 0), axis=1, keepdims=True) & 7
        found = jnp.where(lane == 2 * k, one, jnp.where(lane == 2 * k + 1, two, found))
    table[...] = found
    load = pltpu.make_async_copy(table, picks, table_sem)
    load.start()
    load.wait()
    for axis in (0, 1):
        for part in (0, 1):
            first_step(axis, (1, SIDE - 1)[part], part).wait_recv()
            relay(axis, part).start()

    def pass_on(axis, step, other, turn, k, place):
        return pltpu.make_async_remote_copy(
            src_ref=send.at[axis, step * 2 + other, turn],
            dst_ref=got[axis].at[place, k],
            send_sem=send_sems.at[axis, step * 2 + other, turn],
            recv_sem=recv_sems.at[axis, place, k],
            device_id=at(1 - axis, step, other)[0],
            device_id_type=MESH,
        )

    askers = [(step, other) for step in steps + (0,) for other in (0, 1)]
    for turn in (0,) + tuple(SIDE - step for step in steps):
        for axis in (0, 1):
            k = (along[axis] + turn) % SIDE
            if turn == 2:
                for part in (0, 1):
                    relay(axis, part).wait_recv()
            elif turn:
                first_step(axis, SIDE - turn, int(turn == SIDE - 1)).wait_recv()
            for step, other in askers:
                row = (1 - axis) * places + at(1 - axis, step, other)[1]
                for r in range(REQUESTS):
                    part = held[axis][turn][picks[row, REQUESTS * k + r]]
                    if (step, other) == (0, 0):
                        got[axis][mine[1 - axis], k, r] = part
                    else:
                        send[axis, step * 2 + other, turn, r] = part
                if (step, other) != (0, 0):
                    pass_on(axis, step, other, turn, k, mine[1 - axis]).start()
    pl.semaphore_wait(ready_plane, len(steps))
    for step in steps:
        pl.semaphore_signal(ready_all, inc=1, device_id=across(step), device_id_type=MESH)

    rows_here = patches * patch
    devices = incoming.shape[0]
    loads[2].wait()
    loads[3].wait()
    target = dest[...] >> 9
    on_device = lax.broadcasted_iota(jnp.int32, (devices, rows_here), 0) == target
    before = lax.broadcasted_iota(jnp.int32, (rows_here, rows_here), 0) < lax.broadcasted_iota(
        jnp.int32, (rows_here, rows_here), 1
    )
    earlier = mm(on_device.astype(BF16), before.astype(BF16))
    rank = jnp.sum(jnp.where(on_device, earlier, 0.0), axis=0, keepdims=True)
    slot = target * SLOTS + rank.astype(jnp.int32)
    lane = lax.broadcasted_iota(jnp.int32, (devices, 128), 1)
    place = (dest[...] & 511) + 1
    table_out = jnp.zeros((devices, 128), jnp.int32)
    for j in range(SLOTS):
        here = jnp.where(on_device & (earlier == j), place, 0)
        table_out = jnp.where(lane == j, jnp.sum(here, axis=1, keepdims=True), table_out)
    out_places[...] = table_out.reshape(devices, 1, 128)

    pl.semaphore_wait(ready_all, len(steps))
    group = devices // SIDE
    me = grp * group + seq

    def send_to(source, target, sems, to):
        return pltpu.make_async_remote_copy(
            src_ref=source.at[to],
            dst_ref=target.at[me],
            send_sem=sems.at[0],
            recv_sem=sems.at[1],
            device_id=(to // group, to % group),
            device_id_type=MESH,
        )

    def arrive(source, target, sems):
        blocks = pl.ds(0, devices - 1)
        pltpu.make_async_remote_copy(
            src_ref=source.at[blocks],
            dst_ref=target.at[blocks],
            send_sem=sems.at[0],
            recv_sem=sems.at[1],
            device_id=across(1),
            device_id_type=MESH,
        ).wait()

    def send_places(k, carry):
        send_to(out_places, in_places, place_sems, (me + k) % devices).start()
        return carry

    lax.fori_loop(1, devices, send_places, 0)
    in_places[me] = out_places[me]
    gain = gains[0:1]
    rows = points[...].reshape(rows_here, channels)
    copies[0].wait()
    hidden = norm(rows, gain)
    q_ref[...] = mm(hidden, wq[:, :channels]).astype(BF16)
    kv_ref[...] = mm(hidden, wq[:, channels:]).astype(BF16).reshape(patches, patch, 2 * channels)

    def device_at(dy, n):
        dx, dz, dc = n // (2 * SIDE), (n // 2) % SIDE, n % 2
        number = ((x + dx) % SIDE * SIDE + (z + dz) % SIDE) * 2 + (c + dc) % 2
        return (grp + dy) % SIDE, number

    def far(dy, n):
        return sum(min(d, SIDE - d) for d in (dy, n // (2 * SIDE), (n // 2) % SIDE))

    for dy in range(SIDE):
        row = lax.broadcasted_iota(jnp.int32, (group * SLOTS, 1), 0)
        to_grp, number = device_at(dy, row // SLOTS)
        wanted = (to_grp * group + number) * SLOTS + row % SLOTS
        send_match[dy * group * SLOTS : (dy + 1) * group * SLOTS] = (wanted == slot).astype(BF16)

    for axis in (0, 1):
        for part in (0, 1):
            first_step(axis, 1, part).wait_send()
            first_step(axis, SIDE - 1, part).wait_send()
            relay(axis, part).wait_send()
        for step, other in askers:
            if (step, other) != (0, 0):
                for k in range(SIDE):
                    pass_on(axis, step, other, k, k, at(1 - axis, step, other)[1]).wait()

    owners = []
    for p in range(patches):
        for j in range(pattern.shape[0]):
            owner = named[p * pattern.shape[0] + j] >> 3
            r = jnp.int32(0)
            for earlier_owner in owners:
                r = r + jnp.where(earlier_owner == owner, 1, 0)
            owners.append(owner)
            r = jnp.minimum(r, REQUESTS - 1)
            ox, oz, oc = owner // places, (owner // 2) % SIDE, owner % 2
            to = slice(j * patch, (j + 1) * patch)
            chosen[p, to, :half] = got_x[oz * 2 + oc, ox, r]
            chosen[p, to, half:] = got_z[ox * 2 + oc, oz, r]

    def one(p, carry):
        hidden = norm(chosen[p], gain)
        kv = jnp.concatenate([kv_ref[p], mm(hidden, wq[:, channels:]).astype(BF16)], axis=0)
        start = pl.multiple_of(p * patch, patch)
        att_ref[pl.ds(start, patch)] = attend_patch(
            q_ref[pl.ds(start, patch)], kv[:, :channels], kv[:, channels:]
        )
        return carry

    lax.fori_loop(0, patches, one, 0, unroll=True)
    done = finish(rows, att_ref, gains[1:2], wp, wu, wd, acc_ref, [copy.wait for copy in copies[1:]])

    for dy in range(SIDE):
        outgoing[dy * group : (dy + 1) * group] = (
            mm(send_match[dy * group * SLOTS : (dy + 1) * group * SLOTS], done)
            .astype(BF16)
            .reshape(group, SLOTS, channels)
        )
    for dy, n in sorted([(dy, n) for dy in range(SIDE) for n in range(group)], key=lambda to: -far(*to)):
        if (dy, n) != (0, 0):
            pltpu.make_async_remote_copy(
                src_ref=outgoing.at[dy * group + n],
                dst_ref=incoming.at[me],
                send_sem=row_sems.at[0],
                recv_sem=row_sems.at[1],
                device_id=device_at(dy, n),
                device_id_type=MESH,
            ).start()
    incoming[me] = outgoing[0]

    arrive(out_places, in_places, place_sems)
    slot_place = places_by_slot(in_places[...].reshape(devices, 128))
    step = 128
    for start in range(0, rows_here, step):
        place_of = lax.broadcasted_iota(jnp.int32, (step, devices * SLOTS), 0) + (start + 1)
        recv_match[start : start + step] = (place_of == slot_place).astype(BF16)
    arrive(outgoing, incoming, row_sems)


def second_kernel(
    pattern_hbm, incoming, match, gains_hbm, head_hbm, qkv_hbm, proj_hbm, up_hbm, down_hbm,
    features, normals, pattern, gains, head, rows_ref, q_ref, kv_ref, att_ref, acc_ref, wq, wp, wu, wd, sems, load_sems,
):
    loads = [
        pltpu.make_async_copy(source, target, load_sems.at[n])
        for n, (source, target) in enumerate(
            ((gains_hbm, gains), (head_hbm, head), (pattern_hbm, pattern))
        )
    ]
    copies = weight_copies(1, (qkv_hbm, proj_hbm, up_hbm, down_hbm), (wq, wp, wu, wd), sems)
    for copy in loads + copies:
        copy.start()
    picks, patches = pattern.shape
    rows_here, channels = features.shape
    rows_ref[...] = mm(match[...], incoming[...]).astype(BF16)
    loads[0].wait()
    copies[0].wait()
    hidden = norm(rows_ref[...], gains[2:3])
    q_ref[...] = mm(hidden, wq[:, :channels]).astype(BF16)
    kv_ref[...] = (
        mm(hidden, wq[:, channels:]).astype(BF16).reshape(patches, PATCH, 2 * channels)
    )

    loads[2].wait()

    def one(p, carry):
        kv = jnp.concatenate([kv_ref[p]] + [kv_ref[pattern[j, p]] for j in range(picks)], axis=0)
        at = pl.multiple_of(p * PATCH, PATCH)
        att_ref[pl.ds(at, PATCH)] = attend_patch(
            q_ref[pl.ds(at, PATCH)], kv[:, :channels], kv[:, channels:]
        )
        return carry

    lax.fori_loop(0, patches, one, 0, unroll=True)
    done = finish(
        rows_ref[...], att_ref, gains[3:4], wp, wu, wd, acc_ref, [copy.wait for copy in copies[1:]]
    )
    features[...] = done
    loads[1].wait()
    normals[...] = lax.dot_general(
        head[...], done, (((1,), (1,)), ((), ())), preferred_element_type=F32
    )


def shards(
    points, pattern_first, pattern_second, destination, norm_gains, w_qkv, w_proj, w_up, w_down, w_head
):
    rows_here, channels = points.shape
    patches = rows_here // PATCH
    ff = w_up.shape[2]
    devices = lax.axis_size("grp") * lax.axis_size("seq")
    slots = devices * SLOTS
    vmem = pl.BlockSpec(memory_space=pltpu.VMEM)
    hbm = pl.BlockSpec(memory_space=pltpu.HBM)
    weights = [
        pltpu.VMEM((channels, 3 * channels), BF16),
        pltpu.VMEM((channels, channels), BF16),
        pltpu.VMEM((channels, ff), BF16),
        pltpu.VMEM((ff, channels), BF16),
        pltpu.SemaphoreType.DMA((4,)),
    ]
    params = pltpu.CompilerParams(vmem_limit_bytes=48 << 20)
    work = 2 * rows_here * channels * (4 * channels + 2 * ff)
    cost = pl.CostEstimate(flops=2 * work, bytes_accessed=8 << 20, transcendentals=rows_here * ff)
    places = 2 * SIDE
    half = channels // 2
    keep = lambda array: pltpu.with_memory_space_constraint(array, pltpu.HBM)
    stacks = [keep(array) for array in (w_qkv, w_proj, w_up, w_down)]
    incoming, match = pl.pallas_call(
        first_kernel,
        out_shape=(
            jax.ShapeDtypeStruct((devices, SLOTS, channels), BF16),
            jax.ShapeDtypeStruct((rows_here, slots), BF16),
        ),
        in_specs=[hbm] * 8,
        out_specs=(vmem, vmem),
        scratch_shapes=[
            pltpu.SMEM(pattern_first.shape[::-1], jnp.int32),
            pltpu.VMEM((patches, PATCH, channels), BF16),
            pltpu.VMEM((1, rows_here), jnp.int32),
            pltpu.VMEM(norm_gains.shape, F32),
            pltpu.VMEM((1, 128), jnp.int32),
            pltpu.VMEM((devices, 1, 128), jnp.int32),
            pltpu.VMEM((devices, 1, 128), jnp.int32),
            pltpu.VMEM((slots, rows_here), BF16),
        ]
        + [pltpu.VMEM((patches, PATCH, half), BF16)] * (2 * SIDE)
        + [pltpu.VMEM((places, SIDE, REQUESTS, PATCH, half), BF16)] * 2
        + [
            pltpu.VMEM((2 * places, 1, 128), jnp.int32),
            pltpu.VMEM((2, places, SIDE, REQUESTS, PATCH, half), BF16),
            pltpu.VMEM((2 * places, 128), jnp.int32),
            pltpu.SMEM((2 * places, 128), jnp.int32),
            pltpu.VMEM((patches, pattern_first.shape[1] * PATCH, channels), BF16),
            pltpu.VMEM((rows_here, channels), BF16),
            pltpu.VMEM((patches, PATCH, 2 * channels), BF16),
            pltpu.VMEM((rows_here, channels), BF16),
            pltpu.VMEM((rows_here, channels), F32),
            pltpu.VMEM((devices, SLOTS, channels), BF16),
        ]
        + weights
        + [
            pltpu.SemaphoreType.DMA((2, 2 * places)),
            pltpu.SemaphoreType.DMA((2, 2, SIDE, 2)),
            pltpu.SemaphoreType.DMA((2, places, SIDE)),
            pltpu.SemaphoreType.DMA((2, places, SIDE)),
            pltpu.SemaphoreType.DMA,
            pltpu.SemaphoreType.REGULAR,
            pltpu.SemaphoreType.REGULAR,
            pltpu.SemaphoreType.DMA((4,)),
            pltpu.SemaphoreType.DMA((2,)),
            pltpu.SemaphoreType.DMA((2,)),
        ],
        compiler_params=pltpu.CompilerParams(
            vmem_limit_bytes=48 << 20, collective_id=0, has_side_effects=True
        ),
        cost_estimate=cost,
        name="first_block",
    )(
        keep(pattern_first.T),
        keep(points.reshape(patches, PATCH, channels)),
        keep(destination.reshape(1, rows_here)),
        keep(norm_gains),
        *stacks,
    )
    features, normals = pl.pallas_call(
        second_kernel,
        out_shape=(
            jax.ShapeDtypeStruct((rows_here, channels), BF16),
            jax.ShapeDtypeStruct((w_head.shape[0], rows_here), F32),
        ),
        in_specs=[hbm, vmem, vmem] + [hbm] * 6,
        out_specs=(vmem, vmem),
        scratch_shapes=[
            pltpu.SMEM(pattern_second.shape[::-1], jnp.int32),
            pltpu.VMEM(norm_gains.shape, F32),
            pltpu.VMEM(w_head.shape, BF16),
            pltpu.VMEM((rows_here, channels), BF16),
            pltpu.VMEM((rows_here, channels), BF16),
            pltpu.VMEM((patches, PATCH, 2 * channels), BF16),
            pltpu.VMEM((rows_here, channels), BF16),
            pltpu.VMEM((rows_here, channels), F32),
        ]
        + weights
        + [pltpu.SemaphoreType.DMA((3,))],
        compiler_params=params,
        cost_estimate=cost,
        name="second_block",
    )(
        keep(pattern_second.T),
        incoming.reshape(slots, channels),
        match,
        keep(norm_gains),
        keep(w_head),
        *stacks,
    )
    return features, normals


def solution(mesh):
    split = P(("grp", "seq"))
    return jax.shard_map(
        shards,
        mesh=mesh,
        in_specs=(split, split, split, split) + (P(),) * 6,
        out_specs=(split, P(None, ("grp", "seq"))),
        check_vma=False,
    )
```

```python
import functools

import jax
import jax.numpy as jnp
from jax import lax
from jax.experimental import pallas as pl
from jax.experimental.pallas import tpu as pltpu
from jax.sharding import PartitionSpec as P

HEADS = 8
PATCH = 64
SLOTS = 8
GROUP_HEADS = 4
BF16 = jnp.bfloat16
F32 = jnp.float32
SIDE = 4
REQUESTS = 2
MESH = pl.DeviceIdType.MESH


def norm(rows, gains):
    values = rows.astype(F32)
    centered = values - jnp.mean(values, axis=-1, keepdims=True)
    spread = jnp.mean(centered * centered, axis=-1, keepdims=True)
    return (centered * lax.rsqrt(spread + 1e-05) * gains).astype(BF16)


def mm(a, b):
    return jnp.dot(a, b, preferred_element_type=F32)


def attend_patch(queries, keys, values):
    width = GROUP_HEADS * PATCH
    lane = lax.broadcasted_iota(jnp.int32, (PATCH, width), 1) // PATCH
    mixed = []
    for part in range(HEADS // GROUP_HEADS):
        cols = slice(part * width, (part + 1) * width)
        q = queries[:, cols]
        spread = jnp.concatenate(
            [jnp.where(lane == head, q, jnp.zeros_like(q)) for head in range(GROUP_HEADS)], axis=0
        )
        scores = lax.dot_general(
            spread, keys[:, cols], (((1,), (1,)), ((), ())), preferred_element_type=F32
        )
        top = jnp.max(scores, axis=-1, keepdims=True)
        weights = jnp.exp((scores - top) * PATCH ** (-0.5))
        total = jnp.sum(weights, axis=-1, keepdims=True)
        out = mm(weights.astype(BF16), values[:, cols]) * (1.0 / total)
        acc = jnp.where(lane == 0, out[:PATCH], 0.0)
        for head in range(1, GROUP_HEADS):
            acc = acc + jnp.where(lane == head, out[head * PATCH : (head + 1) * PATCH], 0.0)
        mixed.append(acc)
    return jnp.concatenate(mixed, axis=1).astype(BF16)


def finish(rows, att_ref, gains, wp_ref, wu_ref, wd_ref, acc_ref, waits=()):
    for wait in waits[:1]:
        wait()
    first = (rows.astype(F32) + mm(att_ref[...], wp_ref[...])).astype(BF16)
    hidden = norm(first, gains)
    acc_ref[...] = first.astype(F32)
    for wait in waits[1:]:
        wait()
    ff = wu_ref.shape[1]
    step = 512
    for at in range(0, ff, step):
        upper = mm(hidden, wu_ref[:, at : at + step])
        act = (0.5 * upper * (1.0 + lax.erf(upper * 0.7071067811865476))).astype(BF16)
        acc_ref[...] += mm(act, wd_ref[at : at + step, :])
    return acc_ref[...].astype(BF16)


def weight_copies(block, sources, targets, sems):
    return [
        pltpu.make_async_copy(source.at[block], target, sems.at[n])
        for n, (source, target) in enumerate(zip(sources, targets))
    ]


def places_by_slot(places):
    devices = places.shape[0]
    slots = devices * SLOTS
    table = jnp.transpose(places)[:SLOTS]
    spread = (
        lax.broadcasted_iota(jnp.int32, (devices, slots), 1) // SLOTS
        == lax.broadcasted_iota(jnp.int32, (devices, slots), 0)
    ).astype(BF16)
    high = mm((table >> 4).astype(F32).astype(BF16), spread)
    low = mm((table & 15).astype(F32).astype(BF16), spread)
    of_rank = (
        lax.broadcasted_iota(jnp.int32, (SLOTS, slots), 1) % SLOTS
        == lax.broadcasted_iota(jnp.int32, (SLOTS, slots), 0)
    )
    return jnp.sum(
        jnp.where(of_rank, high * 16.0 + low, 0.0), axis=0, keepdims=True
    ).astype(jnp.int32)


def first_kernel(
    pattern_hbm, points_hbm, dest_hbm, gains_hbm, qkv_hbm, proj_hbm, up_hbm, down_hbm,
    incoming, recv_match, next_wq, next_wp, next_wu, next_wd, pattern, points, dest, gains, asks, out_places, in_places, send_match, hx0, hx1, hx2, hx3, hz0, hz1, hz2, hz3, got_x, got_z, pats, send, table, picks,
    normed, q_ref, kv_ref, att_ref, acc_ref, outgoing, wq, wp, wu, wd, weight_sems, next_sems,
    pat_sems, step_sems, send_sems, recv_sems, table_sem, ready_plane, ready_all, load_sems, row_sems, place_sems,
):
    grp = lax.axis_index("grp")
    seq = lax.axis_index("seq")
    x, z, c = seq // (2 * SIDE), (seq // 2) % SIDE, seq % 2
    patches, patch, channels = points.shape
    half = channels // 2
    places = 2 * SIDE
    rows_here = patches * patch
    loads = [
        pltpu.make_async_copy(source, target, load_sems.at[n])
        for n, (source, target) in enumerate(
            ((pattern_hbm, pattern), (points_hbm, points), (dest_hbm, dest), (gains_hbm, gains))
        )
    ]
    for load in loads:
        load.start()
    stacks = (qkv_hbm, proj_hbm, up_hbm, down_hbm)
    copies = weight_copies(0, stacks, (wq, wp, wu, wd), weight_sems)
    next_copies = weight_copies(1, stacks, (next_wq, next_wp, next_wu, next_wd), next_sems)

    def at(axis, step, other):
        core = (c + other) % 2
        if axis == 0:
            place = (x + step) % SIDE
            return (grp, (place * SIDE + z) * 2 + core), place * 2 + core
        place = (z + step) % SIDE
        return (grp, (x * SIDE + place) * 2 + core), place * 2 + core

    def across(step):
        return ((grp + step) % SIDE, seq)

    peers = [(axis, step, other) for axis in (0, 1) for step in range(SIDE) for other in (0, 1)]
    peers = [peer for peer in peers if peer[1:] != (0, 0)]
    steps = (1, SIDE - 1, 2)
    barrier = pltpu.get_barrier_semaphore()
    for peer in peers:
        pl.semaphore_signal(barrier, inc=1, device_id=at(*peer)[0], device_id_type=MESH)
    for step in steps:
        pl.semaphore_signal(barrier, inc=1, device_id=across(step), device_id_type=MESH)
    for load in loads:
        load.wait()
    rows = points[...].reshape(rows_here, channels)
    normed[...] = norm(rows, gains[0:1]).reshape(patches, patch, channels)
    lane = lax.broadcasted_iota(jnp.int32, asks.shape, 1)
    asking = jnp.full(asks.shape, -1, jnp.int32)
    named = [pattern[j, p] for p in range(patches) for j in range(pattern.shape[0])]
    for n, name in enumerate(named):
        asking = jnp.where(lane == n, name, asking)
    asks[...] = asking
    pl.semaphore_wait(barrier, len(peers) + len(steps))

    along = (x, z)
    mine = (x * 2 + c, z * 2 + c)
    held = ((hx0, hx1, hx2, hx3), (hz0, hz1, hz2, hz3))
    got = (got_x, got_z)

    def half_rows(part):
        return pl.ds(part * (patches // 2), patches // 2)

    def first_step(axis, step, part):
        return pltpu.make_async_remote_copy(
            src_ref=normed.at[half_rows(part), :, pl.ds(axis * half, half)],
            dst_ref=held[axis][SIDE - step].at[half_rows(part)],
            send_sem=step_sems.at[axis, 0, step, part],
            recv_sem=step_sems.at[axis, 1, SIDE - step, part],
            device_id=at(axis, step, 0)[0],
            device_id_type=MESH,
        )

    def relay(axis, part):
        turn, step = ((SIDE - 1, 1), (1, SIDE - 1))[part]
        return pltpu.make_async_remote_copy(
            src_ref=held[axis][turn].at[half_rows(part)],
            dst_ref=held[axis][2].at[half_rows(part)],
            send_sem=step_sems.at[axis, 0, 2, part],
            recv_sem=step_sems.at[axis, 1, 2, part],
            device_id=at(axis, step, 0)[0],
            device_id_type=MESH,
        )

    def ask(axis, step, other, place):
        return pltpu.make_async_remote_copy(
            src_ref=asks,
            dst_ref=pats.at[axis * places + place],
            send_sem=pat_sems.at[0, axis * places + step * 2 + other],
            recv_sem=pat_sems.at[1, axis * places + place],
            device_id=at(axis, step, other)[0],
            device_id_type=MESH,
        )

    for peer in peers:
        ask(*peer, mine[peer[0]]).start()
    for early in (0, 1):
        for axis in (0, 1):
            first_step(axis, 1, early).start()
            first_step(axis, SIDE - 1, 1 - early).start()
    for copy in copies:
        copy.start()
    for step in steps:
        pl.semaphore_signal(ready_plane, inc=1, device_id=at(0, step, 0)[0], device_id_type=MESH)
    for axis in (0, 1):
        held[axis][0][...] = normed[:, :, axis * half : (axis + 1) * half]
        pats[axis * places + mine[axis]] = asks[...]
    for peer in peers:
        ask(*peer, at(*peer)[1]).wait()

    asked = pats[...].reshape(2 * places, pats.shape[2])
    lane = lax.broadcasted_iota(jnp.int32, asked.shape, 1)
    in_row = lax.broadcasted_iota(jnp.int32, asked.shape, 0) < places
    found = jnp.zeros_like(asked)
    for k in range(SIDE):
        source = jnp.where(in_row, (x * SIDE + k) * 2 + c, (k * SIDE + z) * 2 + c)
        match = (asked >> 3) == source
        first = jnp.min(jnp.where(match, lane, asked.shape[1]), axis=1, keepdims=True)
        local = asked & 7
        one = jnp.sum(jnp.where(match & (lane == first), local, 0), axis=1, keepdims=True)
        two = jnp.sum(jnp.where(match & (lane != first), local, 0), axis=1, keepdims=True) & 7
        found = jnp.where(lane == 2 * k, one, jnp.where(lane == 2 * k + 1, two, found))
    table[...] = found
    load = pltpu.make_async_copy(table, picks, table_sem)
    load.start()
    load.wait()
    for axis in (0, 1):
        for part in (0, 1):
            first_step(axis, (1, SIDE - 1)[part], part).wait_recv()
            relay(axis, part).start()

    def pass_on(axis, step, other, turn, k, place):
        return pltpu.make_async_remote_copy(
            src_ref=send.at[axis, step * 2 + other, turn],
            dst_ref=got[axis].at[place, k],
            send_sem=send_sems.at[axis, step * 2 + other, turn],
            recv_sem=recv_sems.at[axis, place, k],
            device_id=at(1 - axis, step, other)[0],
            device_id_type=MESH,
        )

    askers = [(step, other) for step in (2, 1, SIDE - 1, 0) for other in (1, 0)]
    for turn in (0,) + tuple(SIDE - step for step in steps):
        for axis in (0, 1):
            k = (along[axis] + turn) % SIDE
            if turn == 2:
                for part in (0, 1):
                    relay(axis, part).wait_recv()
            elif turn:
                first_step(axis, SIDE - turn, int(turn == SIDE - 1)).wait_recv()
            for step, other in askers:
                row = (1 - axis) * places + at(1 - axis, step, other)[1]
                for r in range(REQUESTS):
                    part = held[axis][turn][picks[row, REQUESTS * k + r]]
                    if (step, other) == (0, 0):
                        got[axis][mine[1 - axis], k, r] = part
                    else:
                        send[axis, step * 2 + other, turn, r] = part
                if (step, other) != (0, 0):
                    pass_on(axis, step, other, turn, k, mine[1 - axis]).start()
    pl.semaphore_wait(ready_plane, len(steps))
    for step in steps:
        pl.semaphore_signal(ready_all, inc=1, device_id=across(step), device_id_type=MESH)

    devices = incoming.shape[0]
    target = dest[...] >> 9
    on_device = lax.broadcasted_iota(jnp.int32, (devices, rows_here), 0) == target
    before = lax.broadcasted_iota(jnp.int32, (rows_here, rows_here), 0) < lax.broadcasted_iota(
        jnp.int32, (rows_here, rows_here), 1
    )
    earlier = mm(on_device.astype(BF16), before.astype(BF16))
    rank = jnp.sum(jnp.where(on_device, earlier, 0.0), axis=0, keepdims=True)
    slot = target * SLOTS + rank.astype(jnp.int32)
    lane = lax.broadcasted_iota(jnp.int32, (devices, 128), 1)
    place = (dest[...] & 511) + 1
    table_out = jnp.zeros((devices, 128), jnp.int32)
    for j in range(SLOTS):
        here = jnp.where(on_device & (earlier == j), place, 0)
        table_out = jnp.where(lane == j, jnp.sum(here, axis=1, keepdims=True), table_out)
    out_places[...] = table_out.reshape(devices, 1, 128)

    pl.semaphore_wait(ready_all, len(steps))
    group = devices // SIDE
    me = grp * group + seq

    def send_to(source, target, sems, to):
        return pltpu.make_async_remote_copy(
            src_ref=source.at[to],
            dst_ref=target.at[me],
            send_sem=sems.at[0],
            recv_sem=sems.at[1],
            device_id=(to // group, to % group),
            device_id_type=MESH,
        )

    def arrive(source, target, sems):
        blocks = pl.ds(0, devices - 1)
        pltpu.make_async_remote_copy(
            src_ref=source.at[blocks],
            dst_ref=target.at[blocks],
            send_sem=sems.at[0],
            recv_sem=sems.at[1],
            device_id=across(1),
            device_id_type=MESH,
        ).wait()

    def send_places(k, carry):
        send_to(out_places, in_places, place_sems, (me + k) % devices).start()
        return carry

    lax.fori_loop(1, devices, send_places, 0)
    in_places[me] = out_places[me]
    copies[0].wait()
    hidden = normed[...].reshape(rows_here, channels)
    q_ref[...] = mm(hidden, wq[:, :channels]).astype(BF16)
    kv_ref[...] = mm(hidden, wq[:, channels:]).astype(BF16).reshape(patches, patch, 2 * channels)
    for copy in next_copies:
        copy.start()

    def device_at(step):
        dy, dx, dz, dc = step
        number = ((x + dx) % SIDE * SIDE + (z + dz) % SIDE) * 2 + (c + dc) % 2
        return (grp + dy) % SIDE, number

    def near(step):
        return -sum(min(d, SIDE - d) for d in step[:3]), step

    ways = range(SIDE)
    order = sorted([(dy, dx, dz, dc) for dy in ways for dx in ways for dz in ways for dc in (0, 1)], key=near)
    order.remove((0, 0, 0, 0))
    order.append((0, 0, 0, 0))
    row = lax.broadcasted_iota(jnp.int32, (2 * SLOTS, rows_here), 0)
    for n in range(0, devices, 2):
        one, two = ((to_grp * group + number) * SLOTS for to_grp, number in map(device_at, order[n : n + 2]))
        wanted = jnp.where(row < SLOTS, one + row, two - SLOTS + row)
        send_match[n * SLOTS : (n + 2) * SLOTS] = (wanted == slot).astype(BF16)

    for axis in (0, 1):
        for part in (0, 1):
            first_step(axis, 1, part).wait_send()
            first_step(axis, SIDE - 1, part).wait_send()
            relay(axis, part).wait_send()
        for step, other in askers:
            if (step, other) != (0, 0):
                for k in range(SIDE):
                    pass_on(axis, step, other, k, k, at(1 - axis, step, other)[1]).wait()

    picks_here = pattern.shape[0]
    owners = []
    for p in range(patches):
        parts = []
        for j in range(picks_here):
            owner = named[p * picks_here + j] >> 3
            r = jnp.int32(0)
            for earlier_owner in owners:
                r = r + jnp.where(earlier_owner == owner, 1, 0)
            owners.append(owner)
            r = jnp.minimum(r, REQUESTS - 1)
            ox, oz, oc = owner // places, (owner // 2) % SIDE, owner % 2
            parts.append(
                jnp.concatenate([got_x[oz * 2 + oc, ox, r], got_z[ox * 2 + oc, oz, r]], axis=1)
            )
        chosen = jnp.concatenate(parts, axis=0)
        kv = jnp.concatenate([kv_ref[p], mm(chosen, wq[:, channels:]).astype(BF16)], axis=0)
        att_ref[p * patch : (p + 1) * patch] = attend_patch(
            q_ref[p * patch : (p + 1) * patch], kv[:, :channels], kv[:, channels:]
        )

    done = finish(rows, att_ref, gains[1:2], wp, wu, wd, acc_ref, [copy.wait for copy in copies[1:]])

    for quarter in range(SIDE):
        start = quarter * group
        outgoing[start : start + group] = (
            mm(send_match[start * SLOTS : (start + group) * SLOTS], done)
            .astype(BF16)
            .reshape(group, SLOTS, channels)
        )
        for n in range(start, min(start + group, devices - 1)):
            pltpu.make_async_remote_copy(
                src_ref=outgoing.at[n],
                dst_ref=incoming.at[me],
                send_sem=row_sems.at[0],
                recv_sem=row_sems.at[1],
                device_id=device_at(order[n]),
                device_id_type=MESH,
            ).start()
    incoming[me] = outgoing[devices - 1]

    arrive(out_places, in_places, place_sems)
    slot_place = places_by_slot(in_places[...].reshape(devices, 128))
    step = 128
    for start in range(0, rows_here, step):
        place_of = lax.broadcasted_iota(jnp.int32, (step, devices * SLOTS), 0) + (start + 1)
        recv_match[start : start + step] = (place_of == slot_place).astype(BF16)
    for copy in next_copies:
        copy.wait()
    arrive(outgoing, incoming, row_sems)


def second_kernel(
    pattern_hbm, incoming, match, gains_hbm, head_hbm, wq, wp, wu, wd,
    features, normals, pattern, gains, head, rows_ref, q_ref, kv_ref, att_ref, acc_ref, load_sems,
):
    loads = [
        pltpu.make_async_copy(source, target, load_sems.at[n])
        for n, (source, target) in enumerate(
            ((gains_hbm, gains), (head_hbm, head), (pattern_hbm, pattern))
        )
    ]
    for load in loads:
        load.start()
    picks, patches = pattern.shape
    rows_here, channels = features.shape
    rows_ref[...] = mm(match[...], incoming[...]).astype(BF16)
    loads[0].wait()
    hidden = norm(rows_ref[...], gains[2:3])
    q_ref[...] = mm(hidden, wq[:, :channels]).astype(BF16)
    kv_ref[...] = (
        mm(hidden, wq[:, channels:]).astype(BF16).reshape(patches, PATCH, 2 * channels)
    )

    loads[2].wait()

    def one(p, carry):
        kv = jnp.concatenate([kv_ref[p]] + [kv_ref[pattern[j, p]] for j in range(picks)], axis=0)
        at = pl.multiple_of(p * PATCH, PATCH)
        att_ref[pl.ds(at, PATCH)] = attend_patch(
            q_ref[pl.ds(at, PATCH)], kv[:, :channels], kv[:, channels:]
        )
        return carry

    lax.fori_loop(0, patches, one, 0, unroll=True)
    done = finish(
        rows_ref[...], att_ref, gains[3:4], wp, wu, wd, acc_ref
    )
    features[...] = done
    loads[1].wait()
    normals[...] = lax.dot_general(
        head[...], done, (((1,), (1,)), ((), ())), preferred_element_type=F32
    )


def shards(
    points, pattern_first, pattern_second, destination, norm_gains, w_qkv, w_proj, w_up, w_down, w_head
):
    rows_here, channels = points.shape
    patches = rows_here // PATCH
    ff = w_up.shape[2]
    devices = lax.axis_size("grp") * lax.axis_size("seq")
    slots = devices * SLOTS
    vmem = pl.BlockSpec(memory_space=pltpu.VMEM)
    hbm = pl.BlockSpec(memory_space=pltpu.HBM)
    weights = [
        pltpu.VMEM((channels, 3 * channels), BF16),
        pltpu.VMEM((channels, channels), BF16),
        pltpu.VMEM((channels, ff), BF16),
        pltpu.VMEM((ff, channels), BF16),
    ]
    params = pltpu.CompilerParams(vmem_limit_bytes=24 << 20)
    work = 2 * rows_here * channels * (4 * channels + 2 * ff)
    cost = pl.CostEstimate(flops=2 * work, bytes_accessed=8 << 20, transcendentals=rows_here * ff)
    places = 2 * SIDE
    half = channels // 2
    keep = lambda array: pltpu.with_memory_space_constraint(array, pltpu.HBM)
    stacks = [keep(array) for array in (w_qkv, w_proj, w_up, w_down)]
    incoming, match, *next_weights = pl.pallas_call(
        first_kernel,
        out_shape=(
            jax.ShapeDtypeStruct((devices, SLOTS, channels), BF16),
            jax.ShapeDtypeStruct((rows_here, slots), BF16),
            *(jax.ShapeDtypeStruct(stack.shape[1:], BF16) for stack in stacks),
        ),
        in_specs=[hbm] * 8,
        out_specs=(vmem,) * 6,
        scratch_shapes=[
            pltpu.SMEM(pattern_first.shape[::-1], jnp.int32),
            pltpu.VMEM((patches, PATCH, channels), BF16),
            pltpu.VMEM((1, rows_here), jnp.int32),
            pltpu.VMEM(norm_gains.shape, F32),
            pltpu.VMEM((1, 128), jnp.int32),
            pltpu.VMEM((devices, 1, 128), jnp.int32),
            pltpu.VMEM((devices, 1, 128), jnp.int32),
            pltpu.VMEM((slots, rows_here), BF16),
        ]
        + [pltpu.VMEM((patches, PATCH, half), BF16)] * (2 * SIDE)
        + [pltpu.VMEM((places, SIDE, REQUESTS, PATCH, half), BF16)] * 2
        + [
            pltpu.VMEM((2 * places, 1, 128), jnp.int32),
            pltpu.VMEM((2, places, SIDE, REQUESTS, PATCH, half), BF16),
            pltpu.VMEM((2 * places, 128), jnp.int32),
            pltpu.SMEM((2 * places, 128), jnp.int32),
            pltpu.VMEM((patches, PATCH, channels), BF16),
            pltpu.VMEM((rows_here, channels), BF16),
            pltpu.VMEM((patches, PATCH, 2 * channels), BF16),
            pltpu.VMEM((rows_here, channels), BF16),
            pltpu.VMEM((rows_here, channels), F32),
            pltpu.VMEM((devices, SLOTS, channels), BF16),
        ]
        + weights
        + [
            pltpu.SemaphoreType.DMA((4,)),
            pltpu.SemaphoreType.DMA((4,)),
            pltpu.SemaphoreType.DMA((2, 2 * places)),
            pltpu.SemaphoreType.DMA((2, 2, SIDE, 2)),
            pltpu.SemaphoreType.DMA((2, places, SIDE)),
            pltpu.SemaphoreType.DMA((2, places, SIDE)),
            pltpu.SemaphoreType.DMA,
            pltpu.SemaphoreType.REGULAR,
            pltpu.SemaphoreType.REGULAR,
            pltpu.SemaphoreType.DMA((4,)),
            pltpu.SemaphoreType.DMA((2,)),
            pltpu.SemaphoreType.DMA((2,)),
        ],
        compiler_params=pltpu.CompilerParams(
            vmem_limit_bytes=32 << 20, collective_id=0, has_side_effects=True
        ),
        cost_estimate=cost,
        name="first_block",
    )(
        keep(pattern_first.T),
        keep(points.reshape(patches, PATCH, channels)),
        keep(destination.reshape(1, rows_here)),
        keep(norm_gains),
        *stacks,
    )
    features, normals = pl.pallas_call(
        second_kernel,
        out_shape=(
            jax.ShapeDtypeStruct((rows_here, channels), BF16),
            jax.ShapeDtypeStruct((w_head.shape[0], rows_here), F32),
        ),
        in_specs=[hbm, vmem, vmem, hbm, hbm] + [vmem] * 4,
        out_specs=(vmem, vmem),
        scratch_shapes=[
            pltpu.SMEM(pattern_second.shape[::-1], jnp.int32),
            pltpu.VMEM(norm_gains.shape, F32),
            pltpu.VMEM(w_head.shape, BF16),
            pltpu.VMEM((rows_here, channels), BF16),
            pltpu.VMEM((rows_here, channels), BF16),
            pltpu.VMEM((patches, PATCH, 2 * channels), BF16),
            pltpu.VMEM((rows_here, channels), BF16),
            pltpu.VMEM((rows_here, channels), F32),
        ]
        + [pltpu.SemaphoreType.DMA((3,))],
        compiler_params=params,
        cost_estimate=cost,
        name="second_block",
    )(
        keep(pattern_second.T),
        incoming.reshape(slots, channels),
        match,
        keep(norm_gains),
        keep(w_head),
        *next_weights,
    )
    return features, normals


def solution(mesh):
    split = P(("grp", "seq"))
    return jax.shard_map(
        shards,
        mesh=mesh,
        in_specs=(split, split, split, split) + (P(),) * 6,
        out_specs=(split, P(None, ("grp", "seq"))),
        check_vma=False,
    )
```

```python
import functools

import jax
import jax.numpy as jnp
from jax import lax
from jax.experimental import pallas as pl
from jax.experimental.pallas import tpu as pltpu
from jax.sharding import PartitionSpec as P

HEADS = 8
PATCH = 64
SLOTS = 8
GROUP_HEADS = 4
BF16 = jnp.bfloat16
F32 = jnp.float32
SIDE = 4
REQUESTS = 2
MESH = pl.DeviceIdType.MESH


def norm(rows, gains):
    values = rows.astype(F32)
    centered = values - jnp.mean(values, axis=-1, keepdims=True)
    spread = jnp.mean(centered * centered, axis=-1, keepdims=True)
    return (centered * lax.rsqrt(spread + 1e-05) * gains).astype(BF16)


def mm(a, b):
    return jnp.dot(a, b, preferred_element_type=F32)


def attend_patch(queries, keys, values):
    width = GROUP_HEADS * PATCH
    lane = lax.broadcasted_iota(jnp.int32, (PATCH, width), 1) // PATCH
    mixed = []
    for part in range(HEADS // GROUP_HEADS):
        cols = slice(part * width, (part + 1) * width)
        q = queries[:, cols]
        spread = jnp.concatenate(
            [jnp.where(lane == head, q, jnp.zeros_like(q)) for head in range(GROUP_HEADS)], axis=0
        )
        scores = lax.dot_general(
            spread, keys[:, cols], (((1,), (1,)), ((), ())), preferred_element_type=F32
        )
        top = jnp.max(scores, axis=-1, keepdims=True)
        weights = jnp.exp((scores - top) * PATCH ** (-0.5))
        total = jnp.sum(weights, axis=-1, keepdims=True)
        out = mm(weights.astype(BF16), values[:, cols]) * (1.0 / total)
        acc = jnp.where(lane == 0, out[:PATCH], 0.0)
        for head in range(1, GROUP_HEADS):
            acc = acc + jnp.where(lane == head, out[head * PATCH : (head + 1) * PATCH], 0.0)
        mixed.append(acc)
    return jnp.concatenate(mixed, axis=1).astype(BF16)


def finish(rows, att_ref, gains, wp_ref, wu_ref, wd_ref, acc_ref, waits=()):
    for wait in waits[:1]:
        wait()
    first = (rows.astype(F32) + mm(att_ref[...], wp_ref[...])).astype(BF16)
    hidden = norm(first, gains)
    acc_ref[...] = first.astype(F32)
    for wait in waits[1:]:
        wait()
    ff = wu_ref.shape[1]
    step = 512
    for at in range(0, ff, step):
        upper = mm(hidden, wu_ref[:, at : at + step])
        act = (0.5 * upper * (1.0 + lax.erf(upper * 0.7071067811865476))).astype(BF16)
        acc_ref[...] += mm(act, wd_ref[at : at + step, :])
    return acc_ref[...].astype(BF16)


def weight_copies(block, sources, targets, sems):
    return [
        pltpu.make_async_copy(source.at[block], target, sems.at[n])
        for n, (source, target) in enumerate(zip(sources, targets))
    ]


def places_by_slot(places):
    devices = places.shape[0]
    slots = devices * SLOTS
    table = jnp.transpose(places)[:SLOTS]
    spread = (
        lax.broadcasted_iota(jnp.int32, (devices, slots), 1) // SLOTS
        == lax.broadcasted_iota(jnp.int32, (devices, slots), 0)
    ).astype(BF16)
    high = mm((table >> 4).astype(F32).astype(BF16), spread)
    low = mm((table & 15).astype(F32).astype(BF16), spread)
    of_rank = (
        lax.broadcasted_iota(jnp.int32, (SLOTS, slots), 1) % SLOTS
        == lax.broadcasted_iota(jnp.int32, (SLOTS, slots), 0)
    )
    return jnp.sum(
        jnp.where(of_rank, high * 16.0 + low, 0.0), axis=0, keepdims=True
    ).astype(jnp.int32)


def first_kernel(
    pattern_hbm, points_hbm, dest_hbm, gains_hbm, qkv_hbm, proj_hbm, up_hbm, down_hbm,
    incoming, recv_match, next_wq, next_wp, next_wu, next_wd, pattern, points, dest, gains, asks, out_places, in_places, send_match, hx0, hx1, hx2, hx3, hz0, hz1, hz2, hz3, got_x, got_z, pats, send, table, picks,
    normed, q_ref, kv_ref, att_ref, acc_ref, outgoing, wq, wp, wu, wd, weight_sems, next_sems,
    pat_sems, step_sems, send_sems, recv_sems, table_sem, ready_plane, ready_all, load_sems, row_sems, place_sems,
):
    grp = lax.axis_index("grp")
    seq = lax.axis_index("seq")
    x, z, c = seq // (2 * SIDE), (seq // 2) % SIDE, seq % 2
    patches, patch, channels = points.shape
    half = channels // 2
    places = 2 * SIDE
    rows_here = patches * patch
    loads = [
        pltpu.make_async_copy(source, target, load_sems.at[n])
        for n, (source, target) in enumerate(
            ((pattern_hbm, pattern), (points_hbm, points), (dest_hbm, dest), (gains_hbm, gains))
        )
    ]
    for load in loads:
        load.start()
    stacks = (qkv_hbm, proj_hbm, up_hbm, down_hbm)
    copies = weight_copies(0, stacks, (wq, wp, wu, wd), weight_sems)
    next_copies = weight_copies(1, stacks, (next_wq, next_wp, next_wu, next_wd), next_sems)

    def at(axis, step, other):
        core = (c + other) % 2
        if axis == 0:
            place = (x + step) % SIDE
            return (grp, (place * SIDE + z) * 2 + core), place * 2 + core
        place = (z + step) % SIDE
        return (grp, (x * SIDE + place) * 2 + core), place * 2 + core

    def across(step):
        return ((grp + step) % SIDE, seq)

    peers = [(axis, step, other) for axis in (0, 1) for step in range(SIDE) for other in (0, 1)]
    peers = [peer for peer in peers if peer[1:] != (0, 0)]
    steps = (1, SIDE - 1, 2)
    barrier = pltpu.get_barrier_semaphore()
    for peer in peers:
        pl.semaphore_signal(barrier, inc=1, device_id=at(*peer)[0], device_id_type=MESH)
    for step in steps:
        pl.semaphore_signal(barrier, inc=1, device_id=across(step), device_id_type=MESH)
    for load in loads:
        load.wait()
    rows = points[...].reshape(rows_here, channels)
    normed[...] = norm(rows, gains[0:1]).reshape(patches, patch, channels)
    lane = lax.broadcasted_iota(jnp.int32, asks.shape, 1)
    asking = jnp.full(asks.shape, -1, jnp.int32)
    named = [pattern[j, p] for p in range(patches) for j in range(pattern.shape[0])]
    for n, name in enumerate(named):
        asking = jnp.where(lane == n, name, asking)
    asks[...] = asking
    pl.semaphore_wait(barrier, len(peers) + len(steps))

    along = (x, z)
    mine = (x * 2 + c, z * 2 + c)
    held = ((hx0, hx1, hx2, hx3), (hz0, hz1, hz2, hz3))
    got = (got_x, got_z)

    def half_rows(part):
        return pl.ds(part * (patches // 2), patches // 2)

    def first_step(axis, step, part):
        return pltpu.make_async_remote_copy(
            src_ref=normed.at[half_rows(part), :, pl.ds(axis * half, half)],
            dst_ref=held[axis][SIDE - step].at[half_rows(part)],
            send_sem=step_sems.at[axis, 0, step, part],
            recv_sem=step_sems.at[axis, 1, SIDE - step, part],
            device_id=at(axis, step, 0)[0],
            device_id_type=MESH,
        )

    def relay(axis, part):
        turn, step = ((SIDE - 1, 1), (1, SIDE - 1))[part]
        return pltpu.make_async_remote_copy(
            src_ref=held[axis][turn].at[half_rows(part)],
            dst_ref=held[axis][2].at[half_rows(part)],
            send_sem=step_sems.at[axis, 0, 2, part],
            recv_sem=step_sems.at[axis, 1, 2, part],
            device_id=at(axis, step, 0)[0],
            device_id_type=MESH,
        )

    def ask(axis, step, other, place):
        return pltpu.make_async_remote_copy(
            src_ref=asks,
            dst_ref=pats.at[axis * places + place],
            send_sem=pat_sems.at[0, axis * places + step * 2 + other],
            recv_sem=pat_sems.at[1, axis * places + place],
            device_id=at(axis, step, other)[0],
            device_id_type=MESH,
        )

    for peer in peers:
        ask(*peer, mine[peer[0]]).start()
    for early in (0, 1):
        for axis in (0, 1):
            first_step(axis, 1, early).start()
            first_step(axis, SIDE - 1, 1 - early).start()
    for copy in copies:
        copy.start()
    for step in steps:
        pl.semaphore_signal(ready_plane, inc=1, device_id=at(0, step, 0)[0], device_id_type=MESH)
    for axis in (0, 1):
        held[axis][0][...] = normed[:, :, axis * half : (axis + 1) * half]
        pats[axis * places + mine[axis]] = asks[...]
    for peer in peers:
        ask(*peer, at(*peer)[1]).wait()

    asked = pats[...].reshape(2 * places, pats.shape[2])
    lane = lax.broadcasted_iota(jnp.int32, asked.shape, 1)
    in_row = lax.broadcasted_iota(jnp.int32, asked.shape, 0) < places
    found = jnp.zeros_like(asked)
    for k in range(SIDE):
        source = jnp.where(in_row, (x * SIDE + k) * 2 + c, (k * SIDE + z) * 2 + c)
        match = (asked >> 3) == source
        first = jnp.min(jnp.where(match, lane, asked.shape[1]), axis=1, keepdims=True)
        local = asked & 7
        one = jnp.sum(jnp.where(match & (lane == first), local, 0), axis=1, keepdims=True)
        two = jnp.sum(jnp.where(match & (lane != first), local, 0), axis=1, keepdims=True) & 7
        found = jnp.where(lane == 2 * k, one, jnp.where(lane == 2 * k + 1, two, found))
    table[...] = found
    load = pltpu.make_async_copy(table, picks, table_sem)
    load.start()
    load.wait()
    for axis in (0, 1):
        for part in (0, 1):
            first_step(axis, (1, SIDE - 1)[part], part).wait_recv()
            relay(axis, part).start()

    def pass_on(axis, step, other, turn, k, place):
        return pltpu.make_async_remote_copy(
            src_ref=send.at[axis, step * 2 + other, turn],
            dst_ref=got[axis].at[place, k],
            send_sem=send_sems.at[axis, step * 2 + other, turn],
            recv_sem=recv_sems.at[axis, place, k],
            device_id=at(1 - axis, step, other)[0],
            device_id_type=MESH,
        )

    askers = [(step, other) for step in (2, 1, SIDE - 1, 0) for other in (1, 0)]
    for turn in (0,) + tuple(SIDE - step for step in steps):
        for axis in (0, 1):
            k = (along[axis] + turn) % SIDE
            if turn == 2:
                for part in (0, 1):
                    relay(axis, part).wait_recv()
            elif turn:
                first_step(axis, SIDE - turn, int(turn == SIDE - 1)).wait_recv()
            for step, other in askers:
                row = (1 - axis) * places + at(1 - axis, step, other)[1]
                for r in range(REQUESTS):
                    part = held[axis][turn][picks[row, REQUESTS * k + r]]
                    if (step, other) == (0, 0):
                        got[axis][mine[1 - axis], k, r] = part
                    else:
                        send[axis, step * 2 + other, turn, r] = part
                if (step, other) != (0, 0):
                    pass_on(axis, step, other, turn, k, mine[1 - axis]).start()
    pl.semaphore_wait(ready_plane, len(steps))
    for step in steps:
        pl.semaphore_signal(ready_all, inc=1, device_id=across(step), device_id_type=MESH)

    devices = incoming.shape[0]
    target = dest[...] >> 9
    on_device = lax.broadcasted_iota(jnp.int32, (devices, rows_here), 0) == target
    before = lax.broadcasted_iota(jnp.int32, (rows_here, rows_here), 0) < lax.broadcasted_iota(
        jnp.int32, (rows_here, rows_here), 1
    )
    earlier = mm(on_device.astype(BF16), before.astype(BF16))
    rank = jnp.sum(jnp.where(on_device, earlier, 0.0), axis=0, keepdims=True)
    slot = target * SLOTS + rank.astype(jnp.int32)
    lane = lax.broadcasted_iota(jnp.int32, (devices, 128), 1)
    place = (dest[...] & 511) + 1
    table_out = jnp.zeros((devices, 128), jnp.int32)
    for j in range(SLOTS):
        here = jnp.where(on_device & (earlier == j), place, 0)
        table_out = jnp.where(lane == j, jnp.sum(here, axis=1, keepdims=True), table_out)
    out_places[...] = table_out.reshape(devices, 1, 128)

    pl.semaphore_wait(ready_all, len(steps))
    group = devices // SIDE
    me = grp * group + seq

    def send_to(source, target, sems, to):
        return pltpu.make_async_remote_copy(
            src_ref=source.at[to],
            dst_ref=target.at[me],
            send_sem=sems.at[0],
            recv_sem=sems.at[1],
            device_id=(to // group, to % group),
            device_id_type=MESH,
        )

    def arrive(source, target, sems):
        blocks = pl.ds(0, devices - 1)
        pltpu.make_async_remote_copy(
            src_ref=source.at[blocks],
            dst_ref=target.at[blocks],
            send_sem=sems.at[0],
            recv_sem=sems.at[1],
            device_id=across(1),
            device_id_type=MESH,
        ).wait()

    def send_places(k, carry):
        send_to(out_places, in_places, place_sems, (me + k) % devices).start()
        return carry

    lax.fori_loop(1, devices, send_places, 0)
    in_places[me] = out_places[me]
    copies[0].wait()
    hidden = normed[...].reshape(rows_here, channels)
    q_ref[...] = mm(hidden, wq[:, :channels]).astype(BF16)
    kv_ref[...] = mm(hidden, wq[:, channels:]).astype(BF16).reshape(patches, patch, 2 * channels)
    for copy in next_copies:
        copy.start()

    def device_at(step):
        dy, dx, dz, dc = step
        number = ((x + dx) % SIDE * SIDE + (z + dz) % SIDE) * 2 + (c + dc) % 2
        return (grp + dy) % SIDE, number

    def near(step):
        return -sum(min(d, SIDE - d) for d in step[:3]), step

    ways = range(SIDE)
    order = sorted([(dy, dx, dz, dc) for dy in ways for dx in ways for dz in ways for dc in (0, 1)], key=near)
    order.remove((0, 0, 0, 0))
    order = [order.pop(0 if n % 4 < 3 else -1) for n in range(len(order))]
    order.append((0, 0, 0, 0))
    row = lax.broadcasted_iota(jnp.int32, (2 * SLOTS, rows_here), 0)
    for n in range(0, devices, 2):
        one, two = ((to_grp * group + number) * SLOTS for to_grp, number in map(device_at, order[n : n + 2]))
        wanted = jnp.where(row < SLOTS, one + row, two - SLOTS + row)
        send_match[n * SLOTS : (n + 2) * SLOTS] = (wanted == slot).astype(BF16)

    for axis in (0, 1):
        for part in (0, 1):
            first_step(axis, 1, part).wait_send()
            first_step(axis, SIDE - 1, part).wait_send()
            relay(axis, part).wait_send()
        for step, other in askers:
            if (step, other) != (0, 0):
                for k in range(SIDE):
                    pass_on(axis, step, other, k, k, at(1 - axis, step, other)[1]).wait()

    picks_here = pattern.shape[0]
    owners = []
    for p in range(patches):
        parts = []
        for j in range(picks_here):
            owner = named[p * picks_here + j] >> 3
            r = jnp.int32(0)
            for earlier_owner in owners:
                r = r + jnp.where(earlier_owner == owner, 1, 0)
            owners.append(owner)
            r = jnp.minimum(r, REQUESTS - 1)
            ox, oz, oc = owner // places, (owner // 2) % SIDE, owner % 2
            parts.append(
                jnp.concatenate([got_x[oz * 2 + oc, ox, r], got_z[ox * 2 + oc, oz, r]], axis=1)
            )
        chosen = jnp.concatenate(parts, axis=0)
        kv = jnp.concatenate([kv_ref[p], mm(chosen, wq[:, channels:]).astype(BF16)], axis=0)
        att_ref[p * patch : (p + 1) * patch] = attend_patch(
            q_ref[p * patch : (p + 1) * patch], kv[:, :channels], kv[:, channels:]
        )

    done = finish(rows, att_ref, gains[1:2], wp, wu, wd, acc_ref, [copy.wait for copy in copies[1:]])

    for quarter in range(SIDE):
        start = quarter * group
        outgoing[start : start + group] = (
            mm(send_match[start * SLOTS : (start + group) * SLOTS], done)
            .astype(BF16)
            .reshape(group, SLOTS, channels)
        )
        for n in range(start, min(start + group, devices - 1)):
            pltpu.make_async_remote_copy(
                src_ref=outgoing.at[n],
                dst_ref=incoming.at[me],
                send_sem=row_sems.at[0],
                recv_sem=row_sems.at[1],
                device_id=device_at(order[n]),
                device_id_type=MESH,
            ).start()
    incoming[me] = outgoing[devices - 1]

    arrive(out_places, in_places, place_sems)
    slot_place = places_by_slot(in_places[...].reshape(devices, 128))
    step = 128
    for start in range(0, rows_here, step):
        place_of = lax.broadcasted_iota(jnp.int32, (step, devices * SLOTS), 0) + (start + 1)
        recv_match[start : start + step] = (place_of == slot_place).astype(BF16)
    for copy in next_copies:
        copy.wait()
    arrive(outgoing, incoming, row_sems)


def second_kernel(
    pattern_hbm, incoming, match, gains_hbm, head_hbm, wq, wp, wu, wd,
    features, normals, pattern, gains, head, rows_ref, q_ref, kv_ref, att_ref, acc_ref, load_sems,
):
    loads = [
        pltpu.make_async_copy(source, target, load_sems.at[n])
        for n, (source, target) in enumerate(
            ((gains_hbm, gains), (head_hbm, head), (pattern_hbm, pattern))
        )
    ]
    for load in loads:
        load.start()
    picks, patches = pattern.shape
    rows_here, channels = features.shape
    rows_ref[...] = mm(match[...], incoming[...]).astype(BF16)
    loads[0].wait()
    hidden = norm(rows_ref[...], gains[2:3])
    q_ref[...] = mm(hidden, wq[:, :channels]).astype(BF16)
    kv_ref[...] = (
        mm(hidden, wq[:, channels:]).astype(BF16).reshape(patches, PATCH, 2 * channels)
    )

    loads[2].wait()

    def one(p, carry):
        kv = jnp.concatenate([kv_ref[p]] + [kv_ref[pattern[j, p]] for j in range(picks)], axis=0)
        at = pl.multiple_of(p * PATCH, PATCH)
        att_ref[pl.ds(at, PATCH)] = attend_patch(
            q_ref[pl.ds(at, PATCH)], kv[:, :channels], kv[:, channels:]
        )
        return carry

    lax.fori_loop(0, patches, one, 0, unroll=True)
    done = finish(
        rows_ref[...], att_ref, gains[3:4], wp, wu, wd, acc_ref
    )
    features[...] = done
    loads[1].wait()
    normals[...] = lax.dot_general(
        head[...], done, (((1,), (1,)), ((), ())), preferred_element_type=F32
    )


def shards(
    points, pattern_first, pattern_second, destination, norm_gains, w_qkv, w_proj, w_up, w_down, w_head
):
    rows_here, channels = points.shape
    patches = rows_here // PATCH
    ff = w_up.shape[2]
    devices = lax.axis_size("grp") * lax.axis_size("seq")
    slots = devices * SLOTS
    vmem = pl.BlockSpec(memory_space=pltpu.VMEM)
    hbm = pl.BlockSpec(memory_space=pltpu.HBM)
    weights = [
        pltpu.VMEM((channels, 3 * channels), BF16),
        pltpu.VMEM((channels, channels), BF16),
        pltpu.VMEM((channels, ff), BF16),
        pltpu.VMEM((ff, channels), BF16),
    ]
    params = pltpu.CompilerParams(vmem_limit_bytes=24 << 20)
    work = 2 * rows_here * channels * (4 * channels + 2 * ff)
    cost = pl.CostEstimate(flops=2 * work, bytes_accessed=8 << 20, transcendentals=rows_here * ff)
    places = 2 * SIDE
    half = channels // 2
    keep = lambda array: pltpu.with_memory_space_constraint(array, pltpu.HBM)
    stacks = [keep(array) for array in (w_qkv, w_proj, w_up, w_down)]
    incoming, match, *next_weights = pl.pallas_call(
        first_kernel,
        out_shape=(
            jax.ShapeDtypeStruct((devices, SLOTS, channels), BF16),
            jax.ShapeDtypeStruct((rows_here, slots), BF16),
            *(jax.ShapeDtypeStruct(stack.shape[1:], BF16) for stack in stacks),
        ),
        in_specs=[hbm] * 8,
        out_specs=(vmem,) * 6,
        scratch_shapes=[
            pltpu.SMEM(pattern_first.shape[::-1], jnp.int32),
            pltpu.VMEM((patches, PATCH, channels), BF16),
            pltpu.VMEM((1, rows_here), jnp.int32),
            pltpu.VMEM(norm_gains.shape, F32),
            pltpu.VMEM((1, 128), jnp.int32),
            pltpu.VMEM((devices, 1, 128), jnp.int32),
            pltpu.VMEM((devices, 1, 128), jnp.int32),
            pltpu.VMEM((slots, rows_here), BF16),
        ]
        + [pltpu.VMEM((patches, PATCH, half), BF16)] * (2 * SIDE)
        + [pltpu.VMEM((places, SIDE, REQUESTS, PATCH, half), BF16)] * 2
        + [
            pltpu.VMEM((2 * places, 1, 128), jnp.int32),
            pltpu.VMEM((2, places, SIDE, REQUESTS, PATCH, half), BF16),
            pltpu.VMEM((2 * places, 128), jnp.int32),
            pltpu.SMEM((2 * places, 128), jnp.int32),
            pltpu.VMEM((patches, PATCH, channels), BF16),
            pltpu.VMEM((rows_here, channels), BF16),
            pltpu.VMEM((patches, PATCH, 2 * channels), BF16),
            pltpu.VMEM((rows_here, channels), BF16),
            pltpu.VMEM((rows_here, channels), F32),
            pltpu.VMEM((devices, SLOTS, channels), BF16),
        ]
        + weights
        + [
            pltpu.SemaphoreType.DMA((4,)),
            pltpu.SemaphoreType.DMA((4,)),
            pltpu.SemaphoreType.DMA((2, 2 * places)),
            pltpu.SemaphoreType.DMA((2, 2, SIDE, 2)),
            pltpu.SemaphoreType.DMA((2, places, SIDE)),
            pltpu.SemaphoreType.DMA((2, places, SIDE)),
            pltpu.SemaphoreType.DMA,
            pltpu.SemaphoreType.REGULAR,
            pltpu.SemaphoreType.REGULAR,
            pltpu.SemaphoreType.DMA((4,)),
            pltpu.SemaphoreType.DMA((2,)),
            pltpu.SemaphoreType.DMA((2,)),
        ],
        compiler_params=pltpu.CompilerParams(
            vmem_limit_bytes=32 << 20, collective_id=0, has_side_effects=True
        ),
        cost_estimate=cost,
        name="first_block",
    )(
        keep(pattern_first.T),
        keep(points.reshape(patches, PATCH, channels)),
        keep(destination.reshape(1, rows_here)),
        keep(norm_gains),
        *stacks,
    )
    features, normals = pl.pallas_call(
        second_kernel,
        out_shape=(
            jax.ShapeDtypeStruct((rows_here, channels), BF16),
            jax.ShapeDtypeStruct((w_head.shape[0], rows_here), F32),
        ),
        in_specs=[hbm, vmem, vmem, hbm, hbm] + [vmem] * 4,
        out_specs=(vmem, vmem),
        scratch_shapes=[
            pltpu.SMEM(pattern_second.shape[::-1], jnp.int32),
            pltpu.VMEM(norm_gains.shape, F32),
            pltpu.VMEM(w_head.shape, BF16),
            pltpu.VMEM((rows_here, channels), BF16),
            pltpu.VMEM((rows_here, channels), BF16),
            pltpu.VMEM((patches, PATCH, 2 * channels), BF16),
            pltpu.VMEM((rows_here, channels), BF16),
            pltpu.VMEM((rows_here, channels), F32),
        ]
        + [pltpu.SemaphoreType.DMA((3,))],
        compiler_params=params,
        cost_estimate=cost,
        name="second_block",
    )(
        keep(pattern_second.T),
        incoming.reshape(slots, channels),
        match,
        keep(norm_gains),
        keep(w_head),
        *next_weights,
    )
    return features, normals


def solution(mesh):
    split = P(("grp", "seq"))
    return jax.shard_map(
        shards,
        mesh=mesh,
        in_specs=(split, split, split, split) + (P(),) * 6,
        out_specs=(split, P(None, ("grp", "seq"))),
        check_vma=False,
    )
```

```python
import functools

import jax
import jax.numpy as jnp
from jax import lax
from jax.experimental import pallas as pl
from jax.experimental.pallas import tpu as pltpu
from jax.sharding import PartitionSpec as P

HEADS = 8
PATCH = 64
SLOTS = 8
GROUP_HEADS = 4
BF16 = jnp.bfloat16
F32 = jnp.float32
SIDE = 4
REQUESTS = 2
MESH = pl.DeviceIdType.MESH


def norm(rows, gains):
    values = rows.astype(F32)
    centered = values - jnp.mean(values, axis=-1, keepdims=True)
    spread = jnp.mean(centered * centered, axis=-1, keepdims=True)
    return (centered * lax.rsqrt(spread + 1e-05) * gains).astype(BF16)


def mm(a, b):
    return jnp.dot(a, b, preferred_element_type=F32)


def attend_patch(queries, keys, values):
    width = GROUP_HEADS * PATCH
    lane = lax.broadcasted_iota(jnp.int32, (PATCH, width), 1) // PATCH
    mixed = []
    for part in range(HEADS // GROUP_HEADS):
        cols = slice(part * width, (part + 1) * width)
        q = queries[:, cols]
        spread = jnp.concatenate(
            [jnp.where(lane == head, q, jnp.zeros_like(q)) for head in range(GROUP_HEADS)], axis=0
        )
        scores = lax.dot_general(
            spread, keys[:, cols], (((1,), (1,)), ((), ())), preferred_element_type=F32
        )
        top = jnp.max(scores, axis=-1, keepdims=True)
        weights = jnp.exp((scores - top) * PATCH ** (-0.5))
        total = jnp.sum(weights, axis=-1, keepdims=True)
        out = mm(weights.astype(BF16), values[:, cols]) * (1.0 / total)
        acc = jnp.where(lane == 0, out[:PATCH], 0.0)
        for head in range(1, GROUP_HEADS):
            acc = acc + jnp.where(lane == head, out[head * PATCH : (head + 1) * PATCH], 0.0)
        mixed.append(acc)
    return jnp.concatenate(mixed, axis=1).astype(BF16)


def finish(rows, att_ref, gains, wp_ref, wu_ref, wd_ref, acc_ref, waits=()):
    for wait in waits[:1]:
        wait()
    first = (rows.astype(F32) + mm(att_ref[...], wp_ref[...])).astype(BF16)
    hidden = norm(first, gains)
    acc_ref[...] = first.astype(F32)
    for wait in waits[1:]:
        wait()
    ff = wu_ref.shape[1]
    step = 512
    for at in range(0, ff, step):
        upper = mm(hidden, wu_ref[:, at : at + step])
        act = (0.5 * upper * (1.0 + lax.erf(upper * 0.7071067811865476))).astype(BF16)
        acc_ref[...] += mm(act, wd_ref[at : at + step, :])
    return acc_ref[...].astype(BF16)


def weight_copies(block, sources, targets, sems):
    return [
        pltpu.make_async_copy(source.at[block], target, sems.at[n])
        for n, (source, target) in enumerate(zip(sources, targets))
    ]


def places_by_slot(places):
    devices = places.shape[0]
    slots = devices * SLOTS
    table = jnp.transpose(places)[:SLOTS]
    spread = (
        lax.broadcasted_iota(jnp.int32, (devices, slots), 1) // SLOTS
        == lax.broadcasted_iota(jnp.int32, (devices, slots), 0)
    ).astype(BF16)
    high = mm((table >> 4).astype(F32).astype(BF16), spread)
    low = mm((table & 15).astype(F32).astype(BF16), spread)
    of_rank = (
        lax.broadcasted_iota(jnp.int32, (SLOTS, slots), 1) % SLOTS
        == lax.broadcasted_iota(jnp.int32, (SLOTS, slots), 0)
    )
    return jnp.sum(
        jnp.where(of_rank, high * 16.0 + low, 0.0), axis=0, keepdims=True
    ).astype(jnp.int32)


def first_kernel(
    pattern_hbm, points_hbm, dest_hbm, gains_hbm, qkv_hbm, proj_hbm, up_hbm, down_hbm,
    incoming, recv_match, next_wq, next_wp, next_wu, next_wd, pattern, points, dest, gains, asks, out_places, in_places, send_match, hx0, hx1, hx2, hx3, hz0, hz1, hz2, hz3, got_x, got_z, pats, send, table, picks,
    normed, q_ref, kv_ref, att_ref, acc_ref, outgoing, wq, wp, wu, wd, weight_sems, next_sems,
    pat_sems, step_sems, send_sems, recv_sems, table_sem, ready_plane, ready_all, load_sems, row_sems, place_sems,
):
    grp = lax.axis_index("grp")
    seq = lax.axis_index("seq")
    x, z, c = seq // (2 * SIDE), (seq // 2) % SIDE, seq % 2
    patches, patch, channels = points.shape
    half = channels // 2
    places = 2 * SIDE
    rows_here = patches * patch
    loads = [
        pltpu.make_async_copy(source, target, load_sems.at[n])
        for n, (source, target) in enumerate(
            ((pattern_hbm, pattern), (points_hbm, points), (dest_hbm, dest), (gains_hbm, gains))
        )
    ]
    for load in loads:
        load.start()
    stacks = (qkv_hbm, proj_hbm, up_hbm, down_hbm)
    copies = weight_copies(0, stacks, (wq, wp, wu, wd), weight_sems)
    next_copies = weight_copies(1, stacks, (next_wq, next_wp, next_wu, next_wd), next_sems)

    def at(axis, step, other):
        core = (c + other) % 2
        if axis == 0:
            place = (x + step) % SIDE
            return (grp, (place * SIDE + z) * 2 + core), place * 2 + core
        place = (z + step) % SIDE
        return (grp, (x * SIDE + place) * 2 + core), place * 2 + core

    def across(step):
        return ((grp + step) % SIDE, seq)

    peers = [(axis, step, other) for axis in (0, 1) for step in range(SIDE) for other in (0, 1)]
    peers = [peer for peer in peers if peer[1:] != (0, 0)]
    steps = (1, SIDE - 1, 2)
    barrier = pltpu.get_barrier_semaphore()
    for peer in peers:
        pl.semaphore_signal(barrier, inc=1, device_id=at(*peer)[0], device_id_type=MESH)
    for step in steps:
        pl.semaphore_signal(barrier, inc=1, device_id=across(step), device_id_type=MESH)
    loads[0].wait()
    lane = lax.broadcasted_iota(jnp.int32, asks.shape, 1)
    asking = jnp.full(asks.shape, -1, jnp.int32)
    named = [pattern[j, p] for p in range(patches) for j in range(pattern.shape[0])]
    for n, name in enumerate(named):
        asking = jnp.where(lane == n, name, asking)
    asks[...] = asking
    pl.semaphore_wait(barrier, len(peers) + len(steps))

    along = (x, z)
    mine = (x * 2 + c, z * 2 + c)
    held = ((hx0, hx1, hx2, hx3), (hz0, hz1, hz2, hz3))
    got = (got_x, got_z)

    def half_rows(part):
        return pl.ds(part * (patches // 2), patches // 2)

    def first_step(axis, step, part):
        return pltpu.make_async_remote_copy(
            src_ref=normed.at[half_rows(part), :, pl.ds(axis * half, half)],
            dst_ref=held[axis][SIDE - step].at[half_rows(part)],
            send_sem=step_sems.at[axis, 0, step, part],
            recv_sem=step_sems.at[axis, 1, SIDE - step, part],
            device_id=at(axis, step, 0)[0],
            device_id_type=MESH,
        )

    def relay(axis, part):
        turn, step = ((SIDE - 1, 1), (1, SIDE - 1))[part]
        return pltpu.make_async_remote_copy(
            src_ref=held[axis][turn].at[half_rows(part)],
            dst_ref=held[axis][2].at[half_rows(part)],
            send_sem=step_sems.at[axis, 0, 2, part],
            recv_sem=step_sems.at[axis, 1, 2, part],
            device_id=at(axis, step, 0)[0],
            device_id_type=MESH,
        )

    def ask(axis, step, other, place):
        return pltpu.make_async_remote_copy(
            src_ref=asks,
            dst_ref=pats.at[axis * places + place],
            send_sem=pat_sems.at[0, axis * places + step * 2 + other],
            recv_sem=pat_sems.at[1, axis * places + place],
            device_id=at(axis, step, other)[0],
            device_id_type=MESH,
        )

    for peer in peers:
        ask(*peer, mine[peer[0]]).start()
    for load in loads[1:]:
        load.wait()
    rows = points[...].reshape(rows_here, channels)
    normed[...] = norm(rows, gains[0:1]).reshape(patches, patch, channels)
    for early in (0, 1):
        for axis in (0, 1):
            first_step(axis, 1, early).start()
            first_step(axis, SIDE - 1, 1 - early).start()
    for copy in copies:
        copy.start()
    for step in steps:
        pl.semaphore_signal(ready_plane, inc=1, device_id=at(0, step, 0)[0], device_id_type=MESH)
    for axis in (0, 1):
        held[axis][0][...] = normed[:, :, axis * half : (axis + 1) * half]
        pats[axis * places + mine[axis]] = asks[...]
    for peer in peers:
        ask(*peer, at(*peer)[1]).wait()

    asked = pats[...].reshape(2 * places, pats.shape[2])
    lane = lax.broadcasted_iota(jnp.int32, asked.shape, 1)
    in_row = lax.broadcasted_iota(jnp.int32, asked.shape, 0) < places
    found = jnp.zeros_like(asked)
    for k in range(SIDE):
        source = jnp.where(in_row, (x * SIDE + k) * 2 + c, (k * SIDE + z) * 2 + c)
        match = (asked >> 3) == source
        first = jnp.min(jnp.where(match, lane, asked.shape[1]), axis=1, keepdims=True)
        local = asked & 7
        one = jnp.sum(jnp.where(match & (lane == first), local, 0), axis=1, keepdims=True)
        two = jnp.sum(jnp.where(match & (lane != first), local, 0), axis=1, keepdims=True) & 7
        found = jnp.where(lane == 2 * k, one, jnp.where(lane == 2 * k + 1, two, found))
    table[...] = found
    load = pltpu.make_async_copy(table, picks, table_sem)
    load.start()
    load.wait()
    for axis in (0, 1):
        for part in (0, 1):
            first_step(axis, (1, SIDE - 1)[part], part).wait_recv()
            relay(axis, part).start()

    def pass_on(axis, step, other, turn, k, place):
        return pltpu.make_async_remote_copy(
            src_ref=send.at[axis, step * 2 + other, turn],
            dst_ref=got[axis].at[place, k],
            send_sem=send_sems.at[axis, step * 2 + other, turn],
            recv_sem=recv_sems.at[axis, place, k],
            device_id=at(1 - axis, step, other)[0],
            device_id_type=MESH,
        )

    askers = [(step, other) for step in (2, 1, SIDE - 1, 0) for other in (1, 0)]
    for turn in (0,) + tuple(SIDE - step for step in steps):
        for axis in (0, 1):
            k = (along[axis] + turn) % SIDE
            if turn == 2:
                for part in (0, 1):
                    relay(axis, part).wait_recv()
            elif turn:
                first_step(axis, SIDE - turn, int(turn == SIDE - 1)).wait_recv()
            for step, other in askers:
                row = (1 - axis) * places + at(1 - axis, step, other)[1]
                for r in range(REQUESTS):
                    part = held[axis][turn][picks[row, REQUESTS * k + r]]
                    if (step, other) == (0, 0):
                        got[axis][mine[1 - axis], k, r] = part
                    else:
                        send[axis, step * 2 + other, turn, r] = part
                if (step, other) != (0, 0):
                    pass_on(axis, step, other, turn, k, mine[1 - axis]).start()
    pl.semaphore_wait(ready_plane, len(steps))
    for step in steps:
        pl.semaphore_signal(ready_all, inc=1, device_id=across(step), device_id_type=MESH)

    devices = incoming.shape[0]
    target = dest[...] >> 9
    on_device = lax.broadcasted_iota(jnp.int32, (devices, rows_here), 0) == target
    before = lax.broadcasted_iota(jnp.int32, (rows_here, rows_here), 0) < lax.broadcasted_iota(
        jnp.int32, (rows_here, rows_here), 1
    )
    earlier = mm(on_device.astype(BF16), before.astype(BF16))
    rank = jnp.sum(jnp.where(on_device, earlier, 0.0), axis=0, keepdims=True)
    slot = target * SLOTS + rank.astype(jnp.int32)
    lane = lax.broadcasted_iota(jnp.int32, (devices, 128), 1)
    place = (dest[...] & 511) + 1
    table_out = jnp.zeros((devices, 128), jnp.int32)
    for j in range(SLOTS):
        here = jnp.where(on_device & (earlier == j), place, 0)
        table_out = jnp.where(lane == j, jnp.sum(here, axis=1, keepdims=True), table_out)
    out_places[...] = table_out.reshape(devices, 1, 128)

    pl.semaphore_wait(ready_all, len(steps))
    group = devices // SIDE
    me = grp * group + seq

    def send_to(source, target, sems, to):
        return pltpu.make_async_remote_copy(
            src_ref=source.at[to],
            dst_ref=target.at[me],
            send_sem=sems.at[0],
            recv_sem=sems.at[1],
            device_id=(to // group, to % group),
            device_id_type=MESH,
        )

    def arrive(source, target, sems):
        blocks = pl.ds(0, devices - 1)
        pltpu.make_async_remote_copy(
            src_ref=source.at[blocks],
            dst_ref=target.at[blocks],
            send_sem=sems.at[0],
            recv_sem=sems.at[1],
            device_id=across(1),
            device_id_type=MESH,
        ).wait()

    def send_places(k, carry):
        send_to(out_places, in_places, place_sems, (me + k) % devices).start()
        return carry

    lax.fori_loop(1, devices, send_places, 0)
    in_places[me] = out_places[me]
    copies[0].wait()
    hidden = normed[...].reshape(rows_here, channels)
    q_ref[...] = mm(hidden, wq[:, :channels]).astype(BF16)
    kv_ref[...] = mm(hidden, wq[:, channels:]).astype(BF16).reshape(patches, patch, 2 * channels)
    for copy in next_copies:
        copy.start()

    def device_at(step):
        dy, dx, dz, dc = step
        number = ((x + dx) % SIDE * SIDE + (z + dz) % SIDE) * 2 + (c + dc) % 2
        return (grp + dy) % SIDE, number

    def near(step):
        return -sum(min(d, SIDE - d) for d in step[:3]), step

    ways = range(SIDE)
    order = sorted([(dy, dx, dz, dc) for dy in ways for dx in ways for dz in ways for dc in (0, 1)], key=near)
    order.remove((0, 0, 0, 0))
    order.append((0, 0, 0, 0))
    row = lax.broadcasted_iota(jnp.int32, (2 * SLOTS, rows_here), 0)
    for n in range(0, devices, 2):
        one, two = ((to_grp * group + number) * SLOTS for to_grp, number in map(device_at, order[n : n + 2]))
        wanted = jnp.where(row < SLOTS, one + row, two - SLOTS + row)
        send_match[n * SLOTS : (n + 2) * SLOTS] = (wanted == slot).astype(BF16)

    for axis in (0, 1):
        for part in (0, 1):
            first_step(axis, 1, part).wait_send()
            first_step(axis, SIDE - 1, part).wait_send()
            relay(axis, part).wait_send()
        for step, other in askers:
            if (step, other) != (0, 0):
                for k in range(SIDE):
                    pass_on(axis, step, other, k, k, at(1 - axis, step, other)[1]).wait()

    picks_here = pattern.shape[0]
    owners = []
    for p in range(patches):
        parts = []
        for j in range(picks_here):
            owner = named[p * picks_here + j] >> 3
            r = jnp.int32(0)
            for earlier_owner in owners:
                r = r + jnp.where(earlier_owner == owner, 1, 0)
            owners.append(owner)
            r = jnp.minimum(r, REQUESTS - 1)
            ox, oz, oc = owner // places, (owner // 2) % SIDE, owner % 2
            parts.append(
                jnp.concatenate([got_x[oz * 2 + oc, ox, r], got_z[ox * 2 + oc, oz, r]], axis=1)
            )
        chosen = jnp.concatenate(parts, axis=0)
        kv = jnp.concatenate([kv_ref[p], mm(chosen, wq[:, channels:]).astype(BF16)], axis=0)
        att_ref[p * patch : (p + 1) * patch] = attend_patch(
            q_ref[p * patch : (p + 1) * patch], kv[:, :channels], kv[:, channels:]
        )

    done = finish(rows, att_ref, gains[1:2], wp, wu, wd, acc_ref, [copy.wait for copy in copies[1:]])

    for quarter in range(SIDE):
        start = quarter * group
        outgoing[start : start + group] = (
            mm(send_match[start * SLOTS : (start + group) * SLOTS], done)
            .astype(BF16)
            .reshape(group, SLOTS, channels)
        )
        for n in range(start, min(start + group, devices - 1)):
            pltpu.make_async_remote_copy(
                src_ref=outgoing.at[n],
                dst_ref=incoming.at[me],
                send_sem=row_sems.at[0],
                recv_sem=row_sems.at[1],
                device_id=device_at(order[n]),
                device_id_type=MESH,
            ).start()
    incoming[me] = outgoing[devices - 1]

    arrive(out_places, in_places, place_sems)
    slot_place = places_by_slot(in_places[...].reshape(devices, 128))
    step = 128
    for start in range(0, rows_here, step):
        place_of = lax.broadcasted_iota(jnp.int32, (step, devices * SLOTS), 0) + (start + 1)
        recv_match[start : start + step] = (place_of == slot_place).astype(BF16)
    for copy in next_copies:
        copy.wait()
    arrive(outgoing, incoming, row_sems)


def second_kernel(
    pattern_hbm, incoming, match, gains_hbm, head_hbm, wq, wp, wu, wd,
    features, normals, pattern, gains, head, rows_ref, q_ref, kv_ref, att_ref, acc_ref, load_sems,
):
    loads = [
        pltpu.make_async_copy(source, target, load_sems.at[n])
        for n, (source, target) in enumerate(
            ((gains_hbm, gains), (head_hbm, head), (pattern_hbm, pattern))
        )
    ]
    for load in loads:
        load.start()
    picks, patches = pattern.shape
    rows_here, channels = features.shape
    rows_ref[...] = mm(match[...], incoming[...]).astype(BF16)
    loads[0].wait()
    hidden = norm(rows_ref[...], gains[2:3])
    q_ref[...] = mm(hidden, wq[:, :channels]).astype(BF16)
    kv_ref[...] = (
        mm(hidden, wq[:, channels:]).astype(BF16).reshape(patches, PATCH, 2 * channels)
    )

    loads[2].wait()

    def one(p, carry):
        kv = jnp.concatenate([kv_ref[p]] + [kv_ref[pattern[j, p]] for j in range(picks)], axis=0)
        at = pl.multiple_of(p * PATCH, PATCH)
        att_ref[pl.ds(at, PATCH)] = attend_patch(
            q_ref[pl.ds(at, PATCH)], kv[:, :channels], kv[:, channels:]
        )
        return carry

    lax.fori_loop(0, patches, one, 0, unroll=True)
    done = finish(
        rows_ref[...], att_ref, gains[3:4], wp, wu, wd, acc_ref
    )
    features[...] = done
    loads[1].wait()
    normals[...] = lax.dot_general(
        head[...], done, (((1,), (1,)), ((), ())), preferred_element_type=F32
    )


def shards(
    points, pattern_first, pattern_second, destination, norm_gains, w_qkv, w_proj, w_up, w_down, w_head
):
    rows_here, channels = points.shape
    patches = rows_here // PATCH
    ff = w_up.shape[2]
    devices = lax.axis_size("grp") * lax.axis_size("seq")
    slots = devices * SLOTS
    vmem = pl.BlockSpec(memory_space=pltpu.VMEM)
    hbm = pl.BlockSpec(memory_space=pltpu.HBM)
    weights = [
        pltpu.VMEM((channels, 3 * channels), BF16),
        pltpu.VMEM((channels, channels), BF16),
        pltpu.VMEM((channels, ff), BF16),
        pltpu.VMEM((ff, channels), BF16),
    ]
    params = pltpu.CompilerParams(vmem_limit_bytes=24 << 20)
    work = 2 * rows_here * channels * (4 * channels + 2 * ff)
    cost = pl.CostEstimate(flops=2 * work, bytes_accessed=8 << 20, transcendentals=rows_here * ff)
    places = 2 * SIDE
    half = channels // 2
    keep = lambda array: pltpu.with_memory_space_constraint(array, pltpu.HBM)
    stacks = [keep(array) for array in (w_qkv, w_proj, w_up, w_down)]
    incoming, match, *next_weights = pl.pallas_call(
        first_kernel,
        out_shape=(
            jax.ShapeDtypeStruct((devices, SLOTS, channels), BF16),
            jax.ShapeDtypeStruct((rows_here, slots), BF16),
            *(jax.ShapeDtypeStruct(stack.shape[1:], BF16) for stack in stacks),
        ),
        in_specs=[hbm] * 8,
        out_specs=(vmem,) * 6,
        scratch_shapes=[
            pltpu.SMEM(pattern_first.shape[::-1], jnp.int32),
            pltpu.VMEM((patches, PATCH, channels), BF16),
            pltpu.VMEM((1, rows_here), jnp.int32),
            pltpu.VMEM(norm_gains.shape, F32),
            pltpu.VMEM((1, 128), jnp.int32),
            pltpu.VMEM((devices, 1, 128), jnp.int32),
            pltpu.VMEM((devices, 1, 128), jnp.int32),
            pltpu.VMEM((slots, rows_here), BF16),
        ]
        + [pltpu.VMEM((patches, PATCH, half), BF16)] * (2 * SIDE)
        + [pltpu.VMEM((places, SIDE, REQUESTS, PATCH, half), BF16)] * 2
        + [
            pltpu.VMEM((2 * places, 1, 128), jnp.int32),
            pltpu.VMEM((2, places, SIDE, REQUESTS, PATCH, half), BF16),
            pltpu.VMEM((2 * places, 128), jnp.int32),
            pltpu.SMEM((2 * places, 128), jnp.int32),
            pltpu.VMEM((patches, PATCH, channels), BF16),
            pltpu.VMEM((rows_here, channels), BF16),
            pltpu.VMEM((patches, PATCH, 2 * channels), BF16),
            pltpu.VMEM((rows_here, channels), BF16),
            pltpu.VMEM((rows_here, channels), F32),
            pltpu.VMEM((devices, SLOTS, channels), BF16),
        ]
        + weights
        + [
            pltpu.SemaphoreType.DMA((4,)),
            pltpu.SemaphoreType.DMA((4,)),
            pltpu.SemaphoreType.DMA((2, 2 * places)),
            pltpu.SemaphoreType.DMA((2, 2, SIDE, 2)),
            pltpu.SemaphoreType.DMA((2, places, SIDE)),
            pltpu.SemaphoreType.DMA((2, places, SIDE)),
            pltpu.SemaphoreType.DMA,
            pltpu.SemaphoreType.REGULAR,
            pltpu.SemaphoreType.REGULAR,
            pltpu.SemaphoreType.DMA((4,)),
            pltpu.SemaphoreType.DMA((2,)),
            pltpu.SemaphoreType.DMA((2,)),
        ],
        compiler_params=pltpu.CompilerParams(
            vmem_limit_bytes=32 << 20, collective_id=0, has_side_effects=True
        ),
        cost_estimate=cost,
        name="first_block",
    )(
        keep(pattern_first.T),
        keep(points.reshape(patches, PATCH, channels)),
        keep(destination.reshape(1, rows_here)),
        keep(norm_gains),
        *stacks,
    )
    features, normals = pl.pallas_call(
        second_kernel,
        out_shape=(
            jax.ShapeDtypeStruct((rows_here, channels), BF16),
            jax.ShapeDtypeStruct((w_head.shape[0], rows_here), F32),
        ),
        in_specs=[hbm, vmem, vmem, hbm, hbm] + [vmem] * 4,
        out_specs=(vmem, vmem),
        scratch_shapes=[
            pltpu.SMEM(pattern_second.shape[::-1], jnp.int32),
            pltpu.VMEM(norm_gains.shape, F32),
            pltpu.VMEM(w_head.shape, BF16),
            pltpu.VMEM((rows_here, channels), BF16),
            pltpu.VMEM((rows_here, channels), BF16),
            pltpu.VMEM((patches, PATCH, 2 * channels), BF16),
            pltpu.VMEM((rows_here, channels), BF16),
            pltpu.VMEM((rows_here, channels), F32),
        ]
        + [pltpu.SemaphoreType.DMA((3,))],
        compiler_params=params,
        cost_estimate=cost,
        name="second_block",
    )(
        keep(pattern_second.T),
        incoming.reshape(slots, channels),
        match,
        keep(norm_gains),
        keep(w_head),
        *next_weights,
    )
    return features, normals


def solution(mesh):
    split = P(("grp", "seq"))
    return jax.shard_map(
        shards,
        mesh=mesh,
        in_specs=(split, split, split, split) + (P(),) * 6,
        out_specs=(split, P(None, ("grp", "seq"))),
        check_vma=False,
    )
```
